32 devices in a mesh: avg: 4 (over x, core), space: 8 (over z, y).
Axes of the slice: x: 2, y: 2, z: 4, core: 2. Of those that a mesh axis runs over, the one named last changes fastest.
Arguments:
- spectral_state: float32 [3, 2, 1024, 1024], P(None, None, 'space', 'avg'), may hold values from -6 to 6
- phase_index: int32 [4], P('avg'), may hold values from 0 to 63
- weight_count: int32 [4], P('avg'), may hold values from 1 to 7
Outputs:
- advanced: float32 [3, 2, 1024, 1024], P(None, None, 'space', 'avg')
The draws below stay inside these ranges and needn't reach their ends.
All inputs are finite; a program needn't handle non-finite values.
Results may differ from the reference program's by a relative error of at most 0.015.
Values may be sent and summed in bfloat16 or wider, within the bound.
A program may use at most 64 MiB of HBM per device.

```python
import jax
import jax.numpy as jnp
from jax import lax

N = 1024
PHASES = 4


def set_ends(drawn, rng, low, largest):
    shape = drawn.shape
    spot = [jax.random.randint(jax.random.fold_in(rng, axis), (), 0, shape[axis]) for axis in range(len(shape))]
    drawn = drawn.at[tuple(spot)].set(low)
    longest = shape.index(max(shape))
    spot[longest] = (spot[longest] + 1) % shape[longest]
    return drawn.at[tuple(spot)].set(largest)


def levels(own_key, dims, shards, low, high):
    factor_of, own = 1.0, jax.random.fold_in(own_key, 6)
    for position, shards_of in shards:
        steps = jnp.exp(jax.random.uniform(jax.random.fold_in(own, position), (shards_of,), jnp.float32, low / len(shards), high / len(shards)))
        factor_of = factor_of * jnp.repeat(steps, dims[position] // shards_of).reshape([-1 if axis == position else 1 for axis in range(len(dims))])
    return factor_of


def scatter_about(own_key, shape, deviation, reach, cuts=(), kind=jnp.bfloat16):
    gain = levels(own_key, shape, cuts, -0.22, 0.18) if cuts else 1.0
    drawn = jax.random.normal(own_key, shape, jnp.float32) * deviation * gain
    return jnp.minimum(jnp.maximum(drawn, -reach), reach).astype(kind)


def setup_inputs(seed: int = 0) -> dict:
    splits = jax.random.split(jax.random.key(seed), 4)
    return {
        "spectral_state": scatter_about(splits[0], (3, 2, N, N), 1.0, 6.0, ((2, 8), (3, 4)), jnp.float32),
        "phase_index": set_ends(jax.random.randint(splits[1], (PHASES,), 0, 64), jax.random.fold_in(splits[1], 1), 0, 63).astype(jnp.int32),
        "weight_count": set_ends(jax.random.randint(splits[2], (PHASES,), 1, 8), jax.random.fold_in(splits[2], 1), 1, 7).astype(jnp.int32),
    }


coriolis = 1.0
wave_speed = 6.0
phase_step = 0.25
time_step = 2.0
weight_scale = 4.0

def wavenumbers(length):
    positions = jnp.arange(length, dtype=jnp.int32)
    shifted = (positions + length // 2) % length - length // 2
    return shifted.astype(jnp.float32) * (2.0 / length)

def wave_operator(fields, wave_rows, wave_columns):
    east_real, north_real, height_real = (fields[0, 0], fields[1, 0], fields[2, 0])
    east_imag, north_imag, height_imag = (fields[0, 1], fields[1, 1], fields[2, 1])
    real_part = jnp.stack([coriolis * north_real + wave_speed * wave_rows * height_imag, -coriolis * east_real + wave_speed * wave_columns * height_imag, wave_speed * (wave_rows * east_imag + wave_columns * north_imag)])
    imag_part = jnp.stack([coriolis * north_imag - wave_speed * wave_rows * height_real, -coriolis * east_imag - wave_speed * wave_columns * height_real, -wave_speed * (wave_rows * east_real + wave_columns * north_real)])
    return jnp.stack([real_part, imag_part], axis=1)

def wave_exponential(fields, wave_rows, wave_columns, phase_value):
    frequency = jnp.sqrt(coriolis * coriolis + wave_speed * wave_speed * (wave_rows * wave_rows + wave_columns * wave_columns))
    sine_term = jnp.sin(frequency * phase_value) / frequency
    cosine_term = (1.0 - jnp.cos(frequency * phase_value)) / (frequency * frequency)
    single = wave_operator(fields, wave_rows, wave_columns)
    double = wave_operator(single, wave_rows, wave_columns)
    return fields + sine_term * single + cosine_term * double

def flux_tendency(spectra, wave_rows, wave_columns):
    real_part, imag_part = (spectra[:, 0], spectra[:, 1])

    def divergence(planes):
        flux_east = jnp.stack([planes[0], planes[1], planes[3]])
        flux_north = jnp.stack([planes[1], planes[2], planes[4]])
        return wave_rows * flux_east + wave_columns * flux_north
    return jnp.stack([divergence(imag_part), -divergence(real_part)], axis=1)

def rounded(values):
    return lax.optimization_barrier(values.astype(jnp.bfloat16)).astype(jnp.float32)

def rounded_complex(values):
    return lax.complex(rounded(values.real), rounded(values.imag))

def reference(spectral_state, phase_index, weight_count):
    wave_table = wavenumbers(N)
    wave_rows = wave_table[:, None]
    wave_columns = wave_table[None, :]
    total_phases = phase_index.shape[0]

    def one_phase(running_sum, inputs):
        sample_index, numerator = inputs
        phase_value = sample_index.astype(jnp.float32) * phase_step
        weight_value = numerator.astype(jnp.float32) / (weight_scale * total_phases)
        rotated = rounded(wave_exponential(spectral_state, wave_rows, wave_columns, phase_value))
        spectral = lax.complex(rotated[:, 0], rotated[:, 1])
        half_done = rounded_complex(jnp.fft.ifft(spectral, axis=2) * N)
        physical = jnp.fft.ifft(half_done, axis=1).real
        east_wind, north_wind, height = (physical[0], physical[1], physical[2])
        products = rounded(jnp.stack([east_wind * east_wind, east_wind * north_wind, north_wind * north_wind, east_wind * height, north_wind * height]))
        forward_half = rounded_complex(jnp.fft.fft(products, axis=1))
        spectra = jnp.fft.fft(forward_half, axis=2) / N
        stacked = jnp.stack([spectra.real, spectra.imag], axis=1)
        tendency = flux_tendency(stacked, wave_rows, wave_columns)
        rotated_back = wave_exponential(tendency, wave_rows, wave_columns, -phase_value)
        return (running_sum + weight_value * rotated_back, None)
    running_sum, unused = lax.scan(one_phase, jnp.zeros(spectral_state.shape, jnp.float32), (phase_index, weight_count))
    return wave_exponential(spectral_state + time_step * running_sum, wave_rows, wave_columns, time_step)
```

```python
import functools

import jax
import jax.numpy as jnp
import ml_dtypes
import numpy as np
from jax import lax
from jax.experimental import pallas as pl
from jax.experimental.pallas import tpu as pltpu
from jax.sharding import PartitionSpec as P

coriolis = 1.0
wave_speed = 6.0
phase_step = 0.25
time_step = 2.0
weight_scale = 4.0


def wave_of(positions, length):
    shifted = (positions + length // 2) % length - length // 2
    return shifted.astype(jnp.float32) * (2.0 / length)


def circle(products, length):
    angles = (products % length) * (2.0 * np.pi / length)
    return np.cos(angles).astype(np.float32), np.sin(angles).astype(np.float32)


def slot_base(slot, slots, half):
    return np.where(slot < slots // 2, 2 * half * slot, 2 * half * (slots - 1 - slot) + half)


def packed_table(length, slots, chunks):
    half = length // (2 * slots)
    rows = slot_base(np.arange(slots), slots, half)[:, None] + np.arange(half)
    cosine, sine = circle(rows[:, :, None] * np.arange(length), length)
    packed = np.stack([cosine, -sine], axis=1)
    packed[0, 1, 0] = circle(length // 2 * np.arange(length), length)[0]
    packed = packed.reshape(slots, 2, chunks, half // chunks, length).transpose(2, 0, 1, 3, 4)
    return packed.reshape(length, length).astype(ml_dtypes.bfloat16)


def turned(first, second):
    (c, s), (d, t) = first, second
    return c * d - s * t, s * d + c * t


def angle_tables(length, width, owners):
    y = np.arange(length)
    return [
        jnp.asarray(np.stack(circle(step * np.arange(count)[:, None] * y, length)))
        for step, count in ((width, owners), (FINE, width // FINE), (1, FINE))
    ]


def wave_operator(fields, kx, ky):
    (er, ei), (nr, ni), (hr, hi) = fields
    cx, cy = wave_speed * kx, wave_speed * ky
    return (
        (coriolis * nr + cx * hi, coriolis * ni - cx * hr),
        (cy * hi - coriolis * er, -coriolis * ei - cy * hr),
        (cx * ei + cy * ni, -(cx * er + cy * nr)),
    )


def wave_factors(kx, ky, phase):
    square = coriolis * coriolis + wave_speed * wave_speed * (kx * kx + ky * ky)
    frequency = jnp.sqrt(square)
    angle = frequency * phase
    return jnp.sin(angle) / frequency, (1.0 - jnp.cos(angle)) / square


def wave_exponential(fields, kx, ky, factors):
    sine, cosine = factors
    single = wave_operator(fields, kx, ky)
    double = wave_operator(single, kx, ky)
    return tuple(
        tuple(w + sine * a + cosine * b for w, a, b in zip(ws, one, two))
        for ws, one, two in zip(fields, single, double)
    )


def planes(fields):
    return tuple((fields[i, 0], fields[i, 1]) for i in range(fields.shape[0]))


MESH = pl.DeviceIdType.MESH
EDGE = 16
FINE = 16


def column(info, t, index):
    return info[t, :, index : index + 1]


def positions():
    g, a = lax.axis_index("space"), lax.axis_index("avg")
    return g, a, a // 2, a % 2


def edge_partner(g, slots):
    aligned = 1 - (g % (slots // 2) + slots // 2 - 1) // (slots // 2)
    return ((slots - g) % slots + aligned * (slots // 2)) % slots


def greet(slots, chips, edges):
    g, a, q, core = positions()
    barrier = pltpu.get_barrier_semaphore()
    peers = [((g + d) % slots, a) for d in range(1, slots)]
    peers += [(g, 2 * q + 1 - core)]
    peers += [(g, 2 * ((q + m) % chips) + core) for m in range(1, chips)]
    if edges:
        across = edge_partner(g, slots)
        peers += [
            (across, 2 * ((q + m) % chips) + (core + c) % 2)
            for c in range(2) for m in range(chips) if c or m
        ]
    for space, avg in peers:
        pl.semaphore_signal(
            barrier, inc=1, device_id={"space": space, "avg": avg}, device_id_type=MESH
        )
    pl.semaphore_wait(barrier, len(peers))


def sending(slots):
    return sorted(range(1, slots), key=lambda d: (-min(d, slots - d), d))


def remote(src, dst, send, recv, space, avg):
    return pltpu.make_async_remote_copy(
        src_ref=src, dst_ref=dst, send_sem=send, recv_sem=recv,
        device_id={"space": space, "avg": avg}, device_id_type=MESH,
    )


DIMS_NT = (((1,), (1,)), ((), ()))


def step_kernel(
    dims, state, into_rows, back_rows, info, ky, own_kx, phase, blocks, steps, fines, packed_hbm, result,
    moved, top, gx, eg, rows_c, rows_s, half, arr, arr_t, grid, products, packed, ct, st, sine, cosine,
    end_sine, end_cosine, fh, ret, lhs, stage, rsin, acc, xs, rx, fin, own, other, edge,
    ex_s, ex_r, eg_s, eg_r, x_s, x_r, c_s, c_r, a_s, a_r, l_s,
    b_s, b_r, m_s, d_s, d_r, y_s, y_r, gv_s, gv_r, le_s, le_r, bring_s,
):
    slots, chips, chunks, hb, width, block = dims
    length, reach = slots * block, block // 2
    g, a, q, core = positions()
    low, high = g < slots // 2, g >= slots // 2
    partner = 2 * q + 1 - core
    across = edge_partner(g, slots)
    side = g // (slots // 2)
    bring = pltpu.make_async_copy(packed_hbm, packed, bring_s)

    for f in range(3):
        for i in range(2):
            plane = state[f, i].astype(jnp.bfloat16)
            top[f, i] = plane[:EDGE]
            picked = jnp.dot(into_rows[side], plane, preferred_element_type=jnp.float32)
            picked = picked.astype(jnp.bfloat16)
            for s in range(2):
                for t in range(chunks):
                    spot = s * reach + t * hb
                    moved[s, t, f, i] = picked[spot : spot + hb]
    greet(slots, chips, True)

    def build_factors(unused):
        for t in range(chunks):
            for s in range(2):
                def one(j, carry, t=t, s=s):
                    span = pl.ds(pl.multiple_of(j * 256, 256), 256)
                    factors = wave_factors(column(info, t, s), ky[:, span], phase[...])
                    sine[t, s, :, span], cosine[t, s, :, span] = factors
                    return carry
                lax.fori_loop(0, length // 256, one, 0)

    def own_factors():
        end_sine[...], end_cosine[...] = wave_factors(own_kx[...], ky[:, :width], time_step)

    def build_tables():
        for c in range(2):
            for m in range(chips):
                owner = 2 * ((q + m) % chips) + (core + c) % 2
                first = (blocks[0, pl.ds(owner, 1), :], blocks[1, pl.ds(owner, 1), :])

                def one(h, carry, j=c * chips + m, first=first):
                    begin = turned(first, (steps[0, pl.ds(h, 1), :], steps[1, pl.ds(h, 1), :]))
                    cos_rows, sin_rows = turned(begin, (fines[0], fines[1]))
                    at = pl.ds(pl.multiple_of(j * width + h * FINE, FINE), FINE)
                    ct[at, :] = cos_rows.astype(jnp.bfloat16)
                    st[at, :] = sin_rows.astype(jnp.bfloat16)
                    return carry
                lax.fori_loop(0, width // FINE, one, 0)

    exchange = [
        remote(moved.at[1, t], gx.at[t, 1, 0, 0], ex_s.at[t], ex_r.at[t], slots - 1 - g, a)
        for t in range(chunks)
    ]
    edges = [
        remote(top, eg.at[c, m], eg_s.at[c, m], eg_r.at[c, m],
               across, 2 * ((q + chips - m) % chips) + (core + c) % 2)
        for c in range(2) for m in range(chips)
    ]

    def mine(t, s):
        return gx.at[t, 1, 0, 0] if s else moved.at[0, t]

    def over_chips(t, s, m):
        return remote(mine(t, s), gx.at[t, s, 0, m], x_s.at[t, s, m], x_r.at[t, s, m],
                      g, 2 * ((q + chips - m) % chips) + core)

    def over_cores(t, s, m):
        source = gx.at[t, s, 0, m] if m else mine(t, s)
        return remote(source, gx.at[t, s, 1, m], c_s.at[t, s, m], c_r.at[t, s, m], g, partner)

    def to_grid(t, d):
        to = (g + d) % slots
        return remote(half.at[t, to], arr.at[t, g], a_s.at[t, d], a_r.at[t, d], to, a)

    exchange[0].start()

    @pl.when(high)
    def _():
        for copy in edges:
            copy.start()
        eg[...] = jnp.zeros_like(eg)

    for t in range(1, chunks):
        exchange[t].start()
    for t in range(chunks):
        for m in range(1, chips):
            over_chips(t, 0, m).start()
        over_cores(t, 0, 0).start()
    bring.start()
    build_factors(0)
    build_tables()
    for t in range(chunks):
        for m in range(1, chips):
            over_chips(t, 0, m).wait_recv()
            over_cores(t, 0, m).start()
    def spread(t):
        exchange[t].wait_recv()
        for m in range(1, chips):
            over_chips(t, 1, m).start()
        over_cores(t, 1, 0).start()

    spread(0)
    for t in range(chunks):
        for m in range(1, chips):
            over_chips(t, 1, m).wait_recv()
            over_cores(t, 1, m).start()
        if t + 1 < chunks:
            spread(t + 1)
        if t == 0:
            @pl.when(low)
            def _():
                for copy in edges:
                    copy.wait_recv()
        for s in range(2):
            for m in range(chips):
                over_cores(t, s, m).wait_recv()
        own_pair = column(info, t, 2) > 0.5
        sign = column(info, t, 3)
        for j in range(2 * chips):
            c, m = divmod(j, chips)
            span = slice(j * width, (j + 1) * width)
            turned_rows = []
            for s in range(2):
                source = moved.at[0, t] if s + j == 0 else gx.at[t, s, c, m]
                fields = [[source[f, i].astype(jnp.float32) for i in range(2)] for f in range(3)]
                if s == 1 and t == 0:
                    put = column(info, t, 4)[:EDGE] > 0.5
                    for f in range(3):
                        for i in range(2):
                            top = jnp.where(put, eg[c, m, f, i].astype(jnp.float32), fields[f][i][:EDGE])
                            fields[f][i] = (
                                jnp.concatenate([top, fields[f][i][EDGE:]], axis=0) if hb > EDGE else top
                            )
                turned_rows.append(wave_exponential(
                    fields, column(info, t, s), ky[:, span], (sine[t, s, :, span], cosine[t, s, :, span])
                ))
            for f in range(3):
                (re0, im0), (re1, im1) = turned_rows[0][f], turned_rows[1][f]
                for i, value in enumerate((
                    jnp.where(own_pair, re0, re0 + re1), jnp.where(own_pair, re1, sign * (im0 - im1))
                )):
                    rows_c[(i * 3 + f) * hb : (i * 3 + f + 1) * hb, span] = value.astype(jnp.bfloat16)
                for i, value in enumerate((
                    jnp.where(own_pair, -im0, -(im0 + im1)), jnp.where(own_pair, -im1, sign * (re0 - re1))
                )):
                    rows_s[(i * 3 + f) * hb : (i * 3 + f + 1) * hb, span] = value.astype(jnp.bfloat16)
        tile = min(length, max(block, 256))
        for y in range(0, length, tile):
            value = (
                jnp.dot(rows_c[...], ct[:, y : y + tile], preferred_element_type=jnp.float32)
                + jnp.dot(rows_s[...], st[:, y : y + tile], preferred_element_type=jnp.float32)
            ).astype(jnp.bfloat16)
            for b in range(tile // block):
                for i in range(2):
                    for f in range(3):
                        half[t, y // block + b, i * hb : (i + 1) * hb, f * block : (f + 1) * block] = (
                            value[(i * 3 + f) * hb : (i * 3 + f + 1) * hb, b * block : (b + 1) * block]
                        )
        for d in sending(slots):
            to_grid(t, d).start()
        pltpu.make_async_copy(half.at[t, g], arr.at[t, g], l_s.at[t]).start()
    def to_rows(t, d):
        to = (g + d) % slots
        return remote(fh.at[t, to], ret.at[t, g], b_s.at[t, d], b_r.at[t, d], to, a)

    def sum_cores(t):
        return remote(stage.at[t, 1], rsin.at[t], d_s.at[t], d_r.at[t], g, partner)

    def sum_chips(t, m):
        return remote(xs.at[t, m], rx.at[t, m], y_s.at[t, m], y_r.at[t, m],
                      g, 2 * ((q + m) % chips) + core)

    def give(t):
        return remote(fin.at[t], other.at[t], gv_s.at[t], gv_r.at[t], slots - 1 - g, a)

    last = remote(fin.at[0, :, :, :EDGE], edge, le_s, le_r, edge_partner(g, slots), a)

    bring.wait()
    for t in range(chunks):
        for d in range(1, slots):
            to_grid(t, d).wait_recv()
        pltpu.make_async_copy(half.at[t, g], arr.at[t, g], l_s.at[t]).wait()
        together = max(1, 128 // (2 * hb))
        for p in range(0, slots, together):
            value = arr[t, p : p + together].astype(jnp.float32)
            value = value.reshape(together * 2 * hb, 3 * block)
            spot = p * 2 * hb
            arr_t[:, spot : spot + together * 2 * hb] = value.T.astype(jnp.bfloat16)
        depth = length // chunks
        for x in range(0, length, 256):
            value = jnp.dot(
                arr_t[...], packed[t * depth : (t + 1) * depth, x : x + 256],
                preferred_element_type=jnp.float32,
            )
            if t:
                value = value + grid[:, x : x + 256]
            if t < chunks - 1:
                grid[:, x : x + 256] = value
            else:
                value = value * (1.0 / length)
                east, north, height = (value[i * block : (i + 1) * block] for i in range(3))
                for k, pair in enumerate((
                    east * east, east * north, north * north, east * height, north * height
                )):
                    products[k * block : (k + 1) * block, x : x + 256] = pair.astype(jnp.bfloat16)
    for t in range(chunks):
        for k in range(0, depth, 256):
            value = lax.dot_general(
                packed[t * depth + k : t * depth + k + 256, :], products[...], DIMS_NT,
                preferred_element_type=jnp.float32,
            ).astype(jnp.bfloat16)
            for n in range(256 // (2 * hb)):
                fh[t, k // (2 * hb) + n] = value[n * 2 * hb : (n + 1) * 2 * hb]
        for d in sending(slots):
            to_rows(t, d).start()
        pltpu.make_async_copy(fh.at[t, g], ret.at[t, g], m_s.at[t]).start()
    own_factors()

    @pl.when(low)
    def _():
        edge[...] = jnp.zeros_like(edge)

    def finish(t):
        for m in range(1, chips):
            sum_chips(t, m).wait_recv()
            acc[...] += rx[t, m].astype(jnp.float32)
        fin[t] = acc[1].astype(jnp.bfloat16)
        give(t).start()
        if t == 0:
            @pl.when(low)
            def _():
                last.start()
        own[t] = acc[0].astype(jnp.bfloat16)

    for t in range(chunks):
        for d in range(1, slots):
            to_rows(t, d).wait_recv()
        pltpu.make_async_copy(fh.at[t, g], ret.at[t, g], m_s.at[t]).wait()
        for p in range(slots):
            for k in range(5):
                lhs[k * 2 * hb : (k + 1) * 2 * hb, p * block : (p + 1) * block] = (
                    ret[t, p, :, k * block : (k + 1) * block]
                )
        own_pair = column(info, t, 2) > 0.5
        sign, scale = column(info, t, 3), column(info, t, 5)
        for j in range(2 * chips):
            c, m = divmod(j, chips)
            span = slice(j * width, (j + 1) * width)
            by_c = lax.dot_general(lhs[...], ct[span, :], DIMS_NT, preferred_element_type=jnp.float32)
            by_s = lax.dot_general(lhs[...], st[span, :], DIMS_NT, preferred_element_type=jnp.float32)

            def part(values, k, i):
                return values[(2 * k + i) * hb : (2 * k + i + 1) * hb]

            for s in range(2):
                turn = scale * sign if s == 0 else -scale * sign
                real, imag = [], []
                for k in range(5):
                    rc, ic = part(by_c, k, 0), part(by_c, k, 1)
                    rs, iz = part(by_s, k, 0), part(by_s, k, 1)
                    real.append(jnp.where(own_pair, scale * (ic if s else rc), scale * rc + turn * iz))
                    imag.append(jnp.where(own_pair, -scale * (iz if s else rs), turn * ic - scale * rs))
                kx, kyj = column(info, t, s), ky[:, span]
                tendency = [
                    (kx * imag[u] + kyj * imag[v], -(kx * real[u] + kyj * real[v]))
                    for u, v in ((0, 1), (1, 2), (3, 4))
                ]
                back = wave_exponential(
                    tendency, kx, kyj, (-sine[t, s, :, span], cosine[t, s, :, span])
                )
                for f in range(3):
                    for i in range(2):
                        stage[t, c, m, s, f, i] = back[f][i].astype(jnp.bfloat16)
        sum_cores(t).start()
        if t:
            finish(t - 1)
        sum_cores(t).wait_recv()
        for m in range(1, chips):
            xs[t, m] = (
                stage[t, 0, m].astype(jnp.float32) + rsin[t, m].astype(jnp.float32)
            ).astype(jnp.bfloat16)
            sum_chips(t, m).start()
        acc[...] = stage[t, 0, 0].astype(jnp.float32) + rsin[t, 0].astype(jnp.float32)
    finish(chunks - 1)
    for t in range(chunks):
        give(t).wait_recv()

    @pl.when(high)
    def _():
        last.wait_recv()

    for t in range(chunks):
        exchange[t].wait_send()
        for s in range(2):
            for m in range(1, chips):
                over_chips(t, s, m).wait_send()
            for m in range(chips):
                over_cores(t, s, m).wait_send()
        for d in range(1, slots):
            to_grid(t, d).wait_send()

    @pl.when(high)
    def _():
        for copy in edges:
            copy.wait_send()


    for t in range(chunks):
        for d in range(1, slots):
            to_rows(t, d).wait_send()
        sum_cores(t).wait_send()
        for m in range(1, chips):
            sum_chips(t, m).wait_send()
        give(t).wait_send()

    @pl.when(low)
    def _():
        last.wait_send()


    for f in range(3):
        for i in range(2):
            rows = jnp.concatenate(
                [own[t, f, i] for t in range(chunks)] + [other[t, f, i] for t in range(chunks)]
                + [edge[f, i]], axis=0,
            )
            averaged = jnp.dot(back_rows[side], rows, preferred_element_type=jnp.float32)
            result[f, i] = state[f, i] + time_step * averaged
    fields = [[result[f, i] for i in range(2)] for f in range(3)]
    advanced = wave_exponential(fields, own_kx[...], ky[:, :width], (end_sine[...], end_cosine[...]))
    for f in range(3):
        for i in range(2):
            result[f, i] = advanced[f][i]


VMEM = pl.BlockSpec(memory_space=pltpu.VMEM)


def per_device(spectral_state, phase_index, weight_count):
    slots, owners = lax.axis_size("space"), lax.axis_size("avg")
    block, width = spectral_state.shape[2:]
    length, half = block * slots, block // 2
    chips = owners // 2
    chunks = max(1, half // CHUNK_ROWS)
    hb = half // chunks
    dims = (slots, chips, chunks, hb, width, block)
    g, a = lax.axis_index("space"), lax.axis_index("avg")
    q, core = a // 2, a % 2
    low = g < slots // 2
    phase = phase_index[0].astype(jnp.float32) * phase_step
    weight = weight_count[0].astype(jnp.float32) / (weight_scale * owners)

    m, c = jnp.arange(chips, dtype=jnp.int32), jnp.arange(2, dtype=jnp.int32)[:, None]
    order = (2 * ((q + m) % chips) + (core + c) % 2).reshape(-1)
    columns = (order[:, None] * width + jnp.arange(width, dtype=jnp.int32)).reshape(1, -1)
    ky = wave_of(columns, length)
    packed = jnp.asarray(packed_table(length, slots, chunks))

    base = jnp.where(low, 2 * half * g, 2 * half * (slots - 1 - g) + half)
    direct = base + jnp.arange(half, dtype=jnp.int32)
    mirror = jnp.where(direct == 0, length // 2, length - direct)
    first = wave_of(jnp.where(low, direct, mirror), length)
    second = wave_of(jnp.where(low, mirror, direct), length)
    ones = jnp.ones((half,), jnp.float32)
    start = (jnp.arange(half) == 0) & low
    info = jnp.stack([
        first, second, (direct == 0).astype(jnp.float32), jnp.where(low, ones, -ones),
        start.astype(jnp.float32), ones * (weight / length), ones, ones,
    ], axis=1).reshape(chunks, hb, 8)
    own_kx = wave_of(g * block + jnp.arange(block, dtype=jnp.int32)[:, None], length)

    r = np.arange(half)
    into = np.zeros((2, 2, half, block), np.float32)
    into[0, 0, r, r] = 1
    into[0, 1, r, half + r] = 1
    into[1, 0, r, half - r] = 1
    into[1, 1, r[1:], block - r[1:]] = 1
    into = jnp.asarray(into.reshape(2, block, block).astype(ml_dtypes.bfloat16))
    back = np.zeros((2, block, 2 * half + EDGE), np.float32)
    back[0, r, r] = 1
    back[0, half + r, half + r] = 1
    back[1, half - r, r] = 1
    back[1, block - r[1:], half + r[1:]] = 1
    back[1, 0, 2 * half] = 1
    back = jnp.asarray(back.astype(ml_dtypes.bfloat16))

    piece = (3, 2, hb, width)
    dma = pltpu.SemaphoreType.DMA
    vmem = lambda *shape: pltpu.VMEM(shape, jnp.bfloat16)
    wide = lambda *shape: pltpu.VMEM(shape, jnp.float32)
    return pl.pallas_call(
        functools.partial(step_kernel, dims),
        out_shape=jax.ShapeDtypeStruct(spectral_state.shape, jnp.float32),
        in_specs=[VMEM] * 10 + [pl.BlockSpec(memory_space=pl.ANY)],
        out_specs=VMEM,
        scratch_shapes=[
            vmem(2, chunks, *piece), vmem(3, 2, EDGE, width),
            vmem(chunks, 2, 2, chips, *piece), vmem(2, chips, 3, 2, EDGE, width),
            vmem(6 * hb, length), vmem(6 * hb, length),
            vmem(chunks, slots, 2 * hb, 3 * block), vmem(chunks, slots, 2 * hb, 3 * block),
            vmem(3 * block, length // chunks), wide(3 * block, length), vmem(5 * block, length),
            vmem(length, length), vmem(length, length), vmem(length, length),
            wide(chunks, 2, hb, length), wide(chunks, 2, hb, length),
            wide(block, width), wide(block, width),
            vmem(chunks, slots, 2 * hb, 5 * block), vmem(chunks, slots, 2 * hb, 5 * block),
            vmem(10 * hb, length),
            vmem(chunks, 2, chips, 2, *piece), vmem(chunks, chips, 2, *piece),
            wide(2, *piece), vmem(chunks, chips, 2, *piece), vmem(chunks, chips, 2, *piece),
            vmem(chunks, *piece), vmem(chunks, *piece), vmem(chunks, *piece),
            vmem(3, 2, EDGE, width),
            dma((chunks,)), dma((chunks,)),
            dma((2, chips)), dma((2, chips)),
            dma((chunks, 2, chips)), dma((chunks, 2, chips)),
            dma((chunks, 2, chips)), dma((chunks, 2, chips)),
            dma((chunks, slots)), dma((chunks, slots)), dma((chunks,)),
            dma((chunks, slots)), dma((chunks, slots)), dma((chunks,)),
            dma((chunks,)), dma((chunks,)),
            dma((chunks, chips)), dma((chunks, chips)),
            dma((chunks,)), dma((chunks,)),
            dma(()), dma(()), dma(()),
        ],
        compiler_params=pltpu.CompilerParams(
            collective_id=0, has_side_effects=True, vmem_limit_bytes=56 * 2**20
        ),
        name="averaged_step",
    )(spectral_state, into, back, info, ky, own_kx, phase.reshape(1, 1),
      *angle_tables(length, width, owners), packed)


def cube_table(length, slots, chunks):
    half = length // (2 * slots)
    rows = half * np.arange(slots)[:, None] + np.arange(half)
    cosine, sine = circle(rows[:, :, None] * np.arange(length), length)
    packed = np.stack([cosine, -sine], axis=1)
    packed[0, 1, 0] = circle(length // 2 * np.arange(length), length)[0]
    packed = packed.reshape(slots, 2, chunks, half // chunks, length).transpose(2, 0, 1, 3, 4)
    return packed.reshape(length, length).astype(ml_dtypes.bfloat16)


def signal_all(barrier, peers):
    for space, avg in peers:
        pl.semaphore_signal(
            barrier, inc=1, device_id={"space": space, "avg": avg}, device_id_type=MESH
        )


def only_row(n, value, rows):
    spot = lax.broadcasted_iota(jnp.int32, (rows, value.shape[-1]), 0)
    return jnp.where(spot == n, jnp.broadcast_to(value, (rows, value.shape[-1])), 0.0)


def cube_kernel(
    dims, state, order_rows, info, ky, own_kx, phase, blocks, steps, fines, packed_hbm, result,
    ph_mine, ph_got, moved, top, gx, eg, rows_c, rows_s, half, arr, arr_t, grid, products, packed,
    ct, st, sine, cosine, end_sine, end_cosine, fh, ret, lhs, stage, rsin, xs, rb, lt, le,
    ph_s, ph_r, x_s, x_r, c_s, c_r, g_s, eg_s, eg_r, a_s, a_r, l_s,
    b_s, b_r, m_s, d_s, d_r, y_s, y_r, k_s, le_s, le_r, bring_s,
):
    slots, chunks, hb, width, block = dims
    length, reach = slots * block, block // 2
    g, a, q, core = positions()
    side = g // (slots // 2)
    pair_block = g + side * (slots - 1 - 2 * g)
    me = 2 * pair_block + q
    mirror = slots - 1 - g
    partner = 2 * q + 1 - core
    low, high = side == 0, side == 1
    bring = pltpu.make_async_copy(packed_hbm, packed, bring_s)

    def place(slot):
        b = slot // 2
        return b + side * (slots - 1 - 2 * b), 2 * (slot % 2) + core

    def chip(m):
        return (q + m) % 2

    top_tile = jnp.zeros((EDGE, width), jnp.float32)
    for f in range(3):
        for i in range(2):
            plane = state[f, i].astype(jnp.bfloat16)
            top_tile = top_tile + only_row(2 * f + i, state[f, i, 0:1, :], EDGE)
            picked = jnp.dot(order_rows[side], plane, preferred_element_type=jnp.float32)
            picked = picked.astype(jnp.bfloat16)
            for h in range(2):
                for t in range(chunks):
                    spot = h * reach + t * hb
                    moved[h, t, f, i] = picked[spot : spot + hb]
    top[...] = top_tile.astype(jnp.bfloat16)
    ph_mine[...] = jnp.broadcast_to(phase[...], ph_mine.shape)

    barrier = pltpu.get_barrier_semaphore()
    near = [place((me + d) % slots) for d in range(1, slots)] + [(g, partner)]
    near += [(mirror, 2 * chip(m) + core) for m in range(2)]
    across = edge_partner(g, slots)
    below = [(across, c) for c in range(2)] + [(slots - 1 - across, c) for c in range(2)]
    source = edge_partner(pair_block, slots)
    above = [(source, c) for c in range(4)]
    signal_all(barrier, near)

    @pl.when(high)
    def _():
        signal_all(barrier, below)

    @pl.when(q == 0)
    def _():
        signal_all(barrier, above)
    pl.semaphore_wait(barrier, len(near) + len(below) * side + len(above) * (1 - q))

    def build_factors():
        turn = chosen_phase()[:, 0:1]
        for t in range(chunks):
            for s in range(2):
                def one(j, carry, t=t, s=s):
                    span = pl.ds(pl.multiple_of(j * 256, 256), 256)
                    factors = wave_factors(column(info, t, s), ky[:, span], turn)
                    sine[t, s, :, span], cosine[t, s, :, span] = factors
                    return carry
                lax.fori_loop(0, length // 256, one, 0)

    def chosen_phase():
        keep = 1.0 - jnp.abs(q - side).astype(jnp.float32)
        return ph_got[0:1] + keep * (ph_mine[0:1] - ph_got[0:1])

    def build_tables():
        for c in range(2):
            for m in range(2):
                owner = 2 * chip(m) + (core + c) % 2
                first = (blocks[0, pl.ds(owner, 1), :], blocks[1, pl.ds(owner, 1), :])

                def one(h, carry, j=c * 2 + m, first=first):
                    begin = turned(first, (steps[0, pl.ds(h, 1), :], steps[1, pl.ds(h, 1), :]))
                    cos_rows, sin_rows = turned(begin, (fines[0], fines[1]))
                    at = pl.ds(pl.multiple_of(j * width + h * FINE, FINE), FINE)
                    ct[at, :] = cos_rows.astype(jnp.bfloat16)
                    st[at, :] = sin_rows.astype(jnp.bfloat16)
                    return carry
                lax.fori_loop(0, width // FINE, one, 0)

    swap_phase = remote(ph_mine, ph_got, ph_s, ph_r, g, 2 * chip(1) + core)

    def bring_own(t):
        return remote(moved.at[chip(1), t], gx.at[t, side, 0, 1], x_s.at[t, 0], x_r.at[t, 0],
                      g, 2 * chip(1) + core)

    def bring_mirror(t, m):
        return remote(moved.at[chip(m), t], gx.at[t, side, 0, m], x_s.at[t, 1 + m], x_r.at[t, 1 + m],
                      mirror, 2 * chip(m) + core)

    def keep_own(t):
        return pltpu.make_async_copy(moved.at[q, t], gx.at[t, side, 0, 0], g_s.at[t])

    def over_cores(t, kind, m):
        role = (1 - side) if kind else side
        piece = gx.at[t, role, 0, m] if kind + m else moved.at[q, t]
        return remote(piece, gx.at[t, role, 1, m], c_s.at[t, kind, m], c_r.at[t, kind, m], g, partner)

    edges = [
        remote(top, eg.at[c, q], eg_s.at[k, c], eg_r.at[c, q], space, (core + c) % 2)
        for k, space in enumerate((across, slots - 1 - across)) for c in range(2)
    ]

    def to_grid(t, d):
        to = (me + d) % slots
        space, avg = place(to)
        return remote(half.at[t, to], arr.at[t, me], a_s.at[t, d], a_r.at[t, d], space, avg)

    def to_rows(t, d):
        to = (me + d) % slots
        space, avg = place(to)
        return remote(fh.at[t, to], ret.at[t, me], b_s.at[t, d], b_r.at[t, d], space, avg)

    def sum_cores(t):
        return remote(stage.at[t, 1], rsin.at[t], d_s.at[t], d_r.at[t], g, partner)

    def give_own(t):
        return remote(xs.at[t, 1, side], rb.at[t, 0, q], y_s.at[t, 0], y_r.at[t, 0],
                      g, 2 * chip(1) + core)

    def give_mirror(t, m):
        return remote(xs.at[t, m, 1 - side], rb.at[t, 1, q], y_s.at[t, 1 + m], y_r.at[t, 1 + m],
                      mirror, 2 * chip(m) + core)

    def give_self(t):
        return pltpu.make_async_copy(xs.at[t, 0, side], rb.at[t, 0, q], k_s.at[t])

    last = [
        remote(lt.at[m], le.at[side], le_s.at[m], le_r.at[side], source, 2 * chip(m) + core)
        for m in range(2)
    ]

    swap_phase.start()

    @pl.when(high)
    def _():
        for copy in edges:
            copy.start()
    for t in range(chunks):
        for m in range(2):
            bring_mirror(t, m).start()
        bring_own(t).start()
        over_cores(t, 0, 0).start()
        keep_own(t).start()
    bring.start()

    @pl.when(q != 0)
    def _():
        eg[...] = jnp.zeros_like(eg)

    @pl.when(low)
    def _():
        le[...] = jnp.zeros_like(le)
    build_tables()
    swap_phase.wait_recv()
    build_factors()
    scale = chosen_phase()[:, 1:2] * (1.0 / length)

    @pl.when(q == 0)
    def _():
        for c in range(2):
            for m in range(2):
                remote(top, eg.at[c, m], eg_s.at[0, c], eg_r.at[c, m], g, partner).wait_recv()

    def rotate(t):
        bring_own(t).wait_recv()
        over_cores(t, 0, 1).start()
        for m in range(2):
            bring_mirror(t, m).wait_recv()
            over_cores(t, 1, m).start()
        keep_own(t).wait()
        for kind in range(2):
            for m in range(2):
                over_cores(t, kind, m).wait_recv()
        own_pair = column(info, t, 2) > 0.5
        for j in range(4):
            c, m = divmod(j, 2)
            span = slice(j * width, (j + 1) * width)
            turned_rows = []
            for s in range(2):
                piece = gx.at[t, s, c, m]
                fields = [[piece[f, i].astype(jnp.float32) for i in range(2)] for f in range(3)]
                if s == 1 and t == 0:
                    put = column(info, t, 3) > 0.5
                    tile = eg[c, m].astype(jnp.float32)
                    for f in range(3):
                        for i in range(2):
                            n = 2 * f + i
                            row = jnp.broadcast_to(tile[n : n + 1], (hb, width))
                            fields[f][i] = jnp.where(put, row, fields[f][i])
                turned_rows.append(wave_exponential(
                    fields, column(info, t, s), ky[:, span], (sine[t, s, :, span], cosine[t, s, :, span])
                ))
            for f in range(3):
                (re0, im0), (re1, im1) = turned_rows[0][f], turned_rows[1][f]
                for i, value in enumerate((
                    jnp.where(own_pair, re0, re0 + re1), jnp.where(own_pair, re1, im0 - im1)
                )):
                    rows_c[(i * 3 + f) * hb : (i * 3 + f + 1) * hb, span] = value.astype(jnp.bfloat16)
                for i, value in enumerate((
                    jnp.where(own_pair, -im0, -(im0 + im1)), jnp.where(own_pair, -im1, re0 - re1)
                )):
                    rows_s[(i * 3 + f) * hb : (i * 3 + f + 1) * hb, span] = value.astype(jnp.bfloat16)
        tile = min(length, max(block, 256))
        for y in range(0, length, tile):
            value = (
                jnp.dot(rows_c[...], ct[:, y : y + tile], preferred_element_type=jnp.float32)
                + jnp.dot(rows_s[...], st[:, y : y + tile], preferred_element_type=jnp.float32)
            ).astype(jnp.bfloat16)
            for b in range(tile // block):
                for i in range(2):
                    for f in range(3):
                        half[t, y // block + b, i * hb : (i + 1) * hb, f * block : (f + 1) * block] = (
                            value[(i * 3 + f) * hb : (i * 3 + f + 1) * hb, b * block : (b + 1) * block]
                        )
        for d in sending(slots):
            to_grid(t, d).start()
        pltpu.make_async_copy(half.at[t, me], arr.at[t, me], l_s.at[t]).start()

    depth = length // chunks

    def on_grid(t):
        for d in range(1, slots):
            to_grid(t, d).wait_recv()
        pltpu.make_async_copy(half.at[t, me], arr.at[t, me], l_s.at[t]).wait()
        together = max(1, 128 // (2 * hb))
        for p in range(0, slots, together):
            value = arr[t, p : p + together].astype(jnp.float32)
            value = value.reshape(together * 2 * hb, 3 * block)
            spot = p * 2 * hb
            arr_t[:, spot : spot + together * 2 * hb] = value.T.astype(jnp.bfloat16)
        for x in range(0, length, 256):
            value = jnp.dot(
                arr_t[...], packed[t * depth : (t + 1) * depth, x : x + 256],
                preferred_element_type=jnp.float32,
            )
            if t:
                value = value + grid[:, x : x + 256]
            if t < chunks - 1:
                grid[:, x : x + 256] = value
            else:
                value = value * (1.0 / length)
                east, north, height = (value[i * block : (i + 1) * block] for i in range(3))
                for k, pair in enumerate((
                    east * east, east * north, north * north, east * height, north * height
                )):
                    products[k * block : (k + 1) * block, x : x + 256] = pair.astype(jnp.bfloat16)

    bring.wait()
    for t in range(chunks):
        rotate(t)
        if t:
            on_grid(t - 1)
    end_sine[...], end_cosine[...] = wave_factors(own_kx[...], ky[:, :width], time_step)
    on_grid(chunks - 1)

    for t in range(chunks):
        for k in range(0, depth, 256):
            value = lax.dot_general(
                packed[t * depth + k : t * depth + k + 256, :], products[...], DIMS_NT,
                preferred_element_type=jnp.float32,
            ).astype(jnp.bfloat16)
            for n in range(256 // (2 * hb)):
                fh[t, k // (2 * hb) + n] = value[n * 2 * hb : (n + 1) * 2 * hb]
        for d in sending(slots):
            to_rows(t, d).start()
        pltpu.make_async_copy(fh.at[t, me], ret.at[t, me], m_s.at[t]).start()

    def pass_on(t):
        sum_cores(t).wait_recv()
        for m in range(2):
            for s in range(2):
                value = stage[t, 0, m, s].astype(jnp.float32) + rsin[t, m, s].astype(jnp.float32)
                xs[t, m, s] = value.astype(jnp.bfloat16)
                if t == 0 and s == 1:
                    tile = jnp.zeros((EDGE, width), jnp.float32)
                    for f in range(3):
                        for i in range(2):
                            tile = tile + only_row(2 * f + i, value[f, i, 0:1], EDGE)
                    lt[m] = tile.astype(jnp.bfloat16)
        for m in range(2):
            give_mirror(t, m).start()
        give_own(t).start()
        give_self(t).start()
        if t == 0:
            @pl.when(q == 0)
            def _():
                for copy in last:
                    copy.start()

    for t in range(chunks):
        for d in range(1, slots):
            to_rows(t, d).wait_recv()
        pltpu.make_async_copy(fh.at[t, me], ret.at[t, me], m_s.at[t]).wait()
        for p in range(slots):
            for k in range(5):
                lhs[k * 2 * hb : (k + 1) * 2 * hb, p * block : (p + 1) * block] = (
                    ret[t, p, :, k * block : (k + 1) * block]
                )
        own_pair = column(info, t, 2) > 0.5
        for j in range(4):
            c, m = divmod(j, 2)
            span = slice(j * width, (j + 1) * width)
            by_c = lax.dot_general(lhs[...], ct[span, :], DIMS_NT, preferred_element_type=jnp.float32)
            by_s = lax.dot_general(lhs[...], st[span, :], DIMS_NT, preferred_element_type=jnp.float32)

            def part(values, k, i):
                return values[(2 * k + i) * hb : (2 * k + i + 1) * hb] * scale

            for s in range(2):
                real, imag = [], []
                for k in range(5):
                    rc, ic = part(by_c, k, 0), part(by_c, k, 1)
                    rs, iz = part(by_s, k, 0), part(by_s, k, 1)
                    real.append(jnp.where(own_pair, (ic if s else rc), (rc - iz if s else rc + iz)))
                    imag.append(jnp.where(own_pair, -(iz if s else rs), (-ic if s else ic) - rs))
                kx, kyj = column(info, t, s), ky[:, span]
                tendency = [
                    (kx * imag[u] + kyj * imag[v], -(kx * real[u] + kyj * real[v]))
                    for u, v in ((0, 1), (1, 2), (3, 4))
                ]
                back = wave_exponential(
                    tendency, kx, kyj, (-sine[t, s, :, span], cosine[t, s, :, span])
                )
                for f in range(3):
                    for i in range(2):
                        stage[t, c, m, s, f, i] = back[f][i].astype(jnp.bfloat16)
        sum_cores(t).start()
        pass_on(t)

    for t in range(chunks):
        bring_own(t).wait_send()
        for m in range(2):
            bring_mirror(t, m).wait_send()
        for kind in range(2):
            for m in range(2):
                over_cores(t, kind, m).wait_send()
        for d in range(1, slots):
            to_grid(t, d).wait_send()
            to_rows(t, d).wait_send()
        sum_cores(t).wait_send()
    swap_phase.wait_send()

    @pl.when(high)
    def _():
        for copy in edges:
            copy.wait_send()
        for k in range(2):
            remote(lt.at[0], le.at[k], le_s.at[0], le_r.at[k], g, partner).wait_recv()

    for t in range(chunks):
        give_own(t).wait_recv()
        for m in range(2):
            give_mirror(t, m).wait_recv()
        give_self(t).wait()

    edge = le[0].astype(jnp.float32) + le[1].astype(jnp.float32)
    for f in range(3):
        for i in range(2):
            pieces = [
                rb[t, 0, h, f, i].astype(jnp.float32) + rb[t, 1, h, f, i].astype(jnp.float32)
                for h in range(2) for t in range(chunks)
            ]
            n = 2 * f + i
            pieces[0] = jnp.where(
                column(info, 0, 4) > 0.5, jnp.broadcast_to(edge[n : n + 1], (hb, width)), pieces[0]
            )
            rows = jnp.concatenate(pieces, axis=0).astype(jnp.bfloat16)
            averaged = jnp.dot(order_rows[side], rows, preferred_element_type=jnp.float32)
            result[f, i] = state[f, i] + time_step * averaged
    fields = [[result[f, i] for i in range(2)] for f in range(3)]
    advanced = wave_exponential(fields, own_kx[...], ky[:, :width], (end_sine[...], end_cosine[...]))
    for f in range(3):
        for i in range(2):
            result[f, i] = advanced[f][i]

    for t in range(chunks):
        give_own(t).wait_send()
        for m in range(2):
            give_mirror(t, m).wait_send()

    @pl.when(q == 0)
    def _():
        for copy in last:
            copy.wait_send()


def cube_step(spectral_state, phase_index, weight_count):
    slots, owners = lax.axis_size("space"), lax.axis_size("avg")
    block, width = spectral_state.shape[2:]
    length, half = block * slots, block // 2
    chunks = max(1, half // CHUNK_ROWS)
    hb = half // chunks
    dims = (slots, chunks, hb, width, block)
    g, a = lax.axis_index("space"), lax.axis_index("avg")
    q, core = a // 2, a % 2
    low = g < slots // 2
    phase = phase_index[0].astype(jnp.float32) * phase_step
    weight = weight_count[0].astype(jnp.float32) / (weight_scale * owners)
    phase = jnp.where(jnp.arange(128) == 0, phase, weight).reshape(1, 128)

    m, c = jnp.arange(2, dtype=jnp.int32), jnp.arange(2, dtype=jnp.int32)[:, None]
    order = (2 * ((q + m) % 2) + (core + c) % 2).reshape(-1)
    columns = (order[:, None] * width + jnp.arange(width, dtype=jnp.int32)).reshape(1, -1)
    ky = wave_of(columns, length)
    packed = jnp.asarray(cube_table(length, slots, chunks))

    base = block * jnp.where(low, g, slots - 1 - g) + half * q
    direct = base + jnp.arange(half, dtype=jnp.int32)
    mirrored = jnp.where(direct == 0, length // 2, length - direct)
    begins = jnp.arange(half) == 0
    zeros = jnp.zeros((half,), jnp.float32)
    info = jnp.stack([
        wave_of(direct, length), wave_of(mirrored, length), (direct == 0).astype(jnp.float32),
        (begins & (q == 0)).astype(jnp.float32), (begins & ~low).astype(jnp.float32),
        zeros, zeros, zeros,
    ], axis=1).reshape(chunks, hb, 8)
    own_kx = wave_of(g * block + jnp.arange(block, dtype=jnp.int32)[:, None], length)

    r = np.arange(block)
    rows = np.zeros((2, block, block), np.float32)
    rows[0, r, r] = 1
    rows[1, r, -r % block] = 1
    rows = jnp.asarray(rows.astype(ml_dtypes.bfloat16))

    piece = (3, 2, hb, width)
    dma = pltpu.SemaphoreType.DMA
    vmem = lambda *shape: pltpu.VMEM(shape, jnp.bfloat16)
    wide = lambda *shape: pltpu.VMEM(shape, jnp.float32)
    return pl.pallas_call(
        functools.partial(cube_kernel, dims),
        out_shape=jax.ShapeDtypeStruct(spectral_state.shape, jnp.float32),
        in_specs=[VMEM] * 9 + [pl.BlockSpec(memory_space=pl.ANY)],
        out_specs=VMEM,
        scratch_shapes=[
            wide(8, 128), wide(8, 128),
            vmem(2, chunks, *piece), vmem(EDGE, width),
            vmem(chunks, 2, 2, 2, *piece), vmem(2, 2, EDGE, width),
            vmem(6 * hb, length), vmem(6 * hb, length),
            vmem(chunks, slots, 2 * hb, 3 * block), vmem(chunks, slots, 2 * hb, 3 * block),
            vmem(3 * block, length // chunks), wide(3 * block, length), vmem(5 * block, length),
            vmem(length, length), vmem(length, length), vmem(length, length),
            wide(chunks, 2, hb, length), wide(chunks, 2, hb, length),
            wide(block, width), wide(block, width),
            vmem(chunks, slots, 2 * hb, 5 * block), vmem(chunks, slots, 2 * hb, 5 * block),
            vmem(10 * hb, length),
            vmem(chunks, 2, 2, 2, *piece), vmem(chunks, 2, 2, *piece),
            vmem(chunks, 2, 2, *piece), vmem(chunks, 2, 2, *piece),
            vmem(2, EDGE, width), vmem(2, EDGE, width),
            dma(()), dma(()),
            dma((chunks, 3)), dma((chunks, 3)),
            dma((chunks, 2, 2)), dma((chunks, 2, 2)), dma((chunks,)),
            dma((2, 2)), dma((2, 2)),
            dma((chunks, slots)), dma((chunks, slots)), dma((chunks,)),
            dma((chunks, slots)), dma((chunks, slots)), dma((chunks,)),
            dma((chunks,)), dma((chunks,)),
            dma((chunks, 3)), dma((chunks, 3)), dma((chunks,)),
            dma((2,)), dma((2,)), dma(()),
        ],
        compiler_params=pltpu.CompilerParams(
            collective_id=0, has_side_effects=True, vmem_limit_bytes=56 * 2**20
        ),
        name="averaged_step",
    )(spectral_state, rows, info, ky, own_kx, phase,
      *angle_tables(length, width, owners), packed)


CHUNK_ROWS = 16


def solution(mesh):
    in_specs = (P(None, None, "space", "avg"), P("avg"), P("avg"))
    out_specs = P(None, None, "space", "avg")
    body = cube_step if mesh.shape["avg"] == 4 else per_device
    return jax.shard_map(
        body, mesh=mesh, in_specs=in_specs, out_specs=out_specs, check_vma=False
    )
```

```python
import functools

import jax
import jax.numpy as jnp
import ml_dtypes
import numpy as np
from jax import lax
from jax.experimental import pallas as pl
from jax.experimental.pallas import tpu as pltpu
from jax.sharding import PartitionSpec as P

coriolis = 1.0
wave_speed = 6.0
phase_step = 0.25
time_step = 2.0
weight_scale = 4.0


def wave_of(positions, length):
    shifted = (positions + length // 2) % length - length // 2
    return shifted.astype(jnp.float32) * (2.0 / length)


def circle(products, length):
    angles = (products % length) * (2.0 * np.pi / length)
    return np.cos(angles).astype(np.float32), np.sin(angles).astype(np.float32)


def slot_base(slot, slots, half):
    return np.where(slot < slots // 2, 2 * half * slot, 2 * half * (slots - 1 - slot) + half)


def packed_table(length, slots, chunks):
    half = length // (2 * slots)
    rows = slot_base(np.arange(slots), slots, half)[:, None] + np.arange(half)
    cosine, sine = circle(rows[:, :, None] * np.arange(length), length)
    packed = np.stack([cosine, -sine], axis=1)
    packed[0, 1, 0] = circle(length // 2 * np.arange(length), length)[0]
    packed = packed.reshape(slots, 2, chunks, half // chunks, length).transpose(2, 0, 1, 3, 4)
    return packed.reshape(length, length).astype(ml_dtypes.bfloat16)


def turned(first, second):
    (c, s), (d, t) = first, second
    return c * d - s * t, s * d + c * t


def angle_tables(length, width, owners):
    y = np.arange(length)
    return [
        jnp.asarray(np.stack(circle(step * np.arange(count)[:, None] * y, length)))
        for step, count in ((width, owners), (FINE, width // FINE), (1, FINE))
    ]


def wave_operator(fields, kx, ky):
    (er, ei), (nr, ni), (hr, hi) = fields
    cx, cy = wave_speed * kx, wave_speed * ky
    return (
        (coriolis * nr + cx * hi, coriolis * ni - cx * hr),
        (cy * hi - coriolis * er, -coriolis * ei - cy * hr),
        (cx * ei + cy * ni, -(cx * er + cy * nr)),
    )


def wave_factors(kx, ky, phase):
    square = coriolis * coriolis + wave_speed * wave_speed * (kx * kx + ky * ky)
    frequency = jnp.sqrt(square)
    angle = frequency * phase
    return jnp.sin(angle) / frequency, (1.0 - jnp.cos(angle)) / square


def wave_exponential(fields, kx, ky, factors):
    sine, cosine = factors
    single = wave_operator(fields, kx, ky)
    double = wave_operator(single, kx, ky)
    return tuple(
        tuple(w + sine * a + cosine * b for w, a, b in zip(ws, one, two))
        for ws, one, two in zip(fields, single, double)
    )


def planes(fields):
    return tuple((fields[i, 0], fields[i, 1]) for i in range(fields.shape[0]))


MESH = pl.DeviceIdType.MESH
EDGE = 16
FINE = 16


def column(info, t, index):
    return info[t, :, index : index + 1]


def positions():
    g, a = lax.axis_index("space"), lax.axis_index("avg")
    return g, a, a // 2, a % 2


def edge_partner(g, slots):
    aligned = 1 - (g % (slots // 2) + slots // 2 - 1) // (slots // 2)
    return ((slots - g) % slots + aligned * (slots // 2)) % slots


def greet(slots, chips, edges):
    g, a, q, core = positions()
    barrier = pltpu.get_barrier_semaphore()
    peers = [((g + d) % slots, a) for d in range(1, slots)]
    peers += [(g, 2 * q + 1 - core)]
    peers += [(g, 2 * ((q + m) % chips) + core) for m in range(1, chips)]
    if edges:
        across = edge_partner(g, slots)
        peers += [
            (across, 2 * ((q + m) % chips) + (core + c) % 2)
            for c in range(2) for m in range(chips) if c or m
        ]
    for space, avg in peers:
        pl.semaphore_signal(
            barrier, inc=1, device_id={"space": space, "avg": avg}, device_id_type=MESH
        )
    pl.semaphore_wait(barrier, len(peers))


def sending(slots):
    return sorted(range(1, slots), key=lambda d: (-min(d, slots - d), d))


def remote(src, dst, send, recv, space, avg):
    return pltpu.make_async_remote_copy(
        src_ref=src, dst_ref=dst, send_sem=send, recv_sem=recv,
        device_id={"space": space, "avg": avg}, device_id_type=MESH,
    )


DIMS_NT = (((1,), (1,)), ((), ()))


def step_kernel(
    dims, state, into_rows, back_rows, info, ky, own_kx, phase, blocks, steps, fines, packed_hbm, result,
    moved, top, gx, eg, rows_c, rows_s, half, arr, arr_t, grid, products, packed, ct, st, sine, cosine,
    end_sine, end_cosine, fh, ret, lhs, stage, rsin, acc, xs, rx, fin, own, other, edge,
    ex_s, ex_r, eg_s, eg_r, x_s, x_r, c_s, c_r, a_s, a_r, l_s,
    b_s, b_r, m_s, d_s, d_r, y_s, y_r, gv_s, gv_r, le_s, le_r, bring_s,
):
    slots, chips, chunks, hb, width, block = dims
    length, reach = slots * block, block // 2
    g, a, q, core = positions()
    low, high = g < slots // 2, g >= slots // 2
    partner = 2 * q + 1 - core
    across = edge_partner(g, slots)
    side = g // (slots // 2)
    bring = pltpu.make_async_copy(packed_hbm, packed, bring_s)

    for f in range(3):
        for i in range(2):
            plane = state[f, i].astype(jnp.bfloat16)
            top[f, i] = plane[:EDGE]
            picked = jnp.dot(into_rows[side], plane, preferred_element_type=jnp.float32)
            picked = picked.astype(jnp.bfloat16)
            for s in range(2):
                for t in range(chunks):
                    spot = s * reach + t * hb
                    moved[s, t, f, i] = picked[spot : spot + hb]
    greet(slots, chips, True)

    def build_factors(unused):
        for t in range(chunks):
            for s in range(2):
                def one(j, carry, t=t, s=s):
                    span = pl.ds(pl.multiple_of(j * 256, 256), 256)
                    factors = wave_factors(column(info, t, s), ky[:, span], phase[...])
                    sine[t, s, :, span], cosine[t, s, :, span] = factors
                    return carry
                lax.fori_loop(0, length // 256, one, 0)

    def own_factors():
        end_sine[...], end_cosine[...] = wave_factors(own_kx[...], ky[:, :width], time_step)

    def build_tables():
        for c in range(2):
            for m in range(chips):
                owner = 2 * ((q + m) % chips) + (core + c) % 2
                first = (blocks[0, pl.ds(owner, 1), :], blocks[1, pl.ds(owner, 1), :])

                def one(h, carry, j=c * chips + m, first=first):
                    begin = turned(first, (steps[0, pl.ds(h, 1), :], steps[1, pl.ds(h, 1), :]))
                    cos_rows, sin_rows = turned(begin, (fines[0], fines[1]))
                    at = pl.ds(pl.multiple_of(j * width + h * FINE, FINE), FINE)
                    ct[at, :] = cos_rows.astype(jnp.bfloat16)
                    st[at, :] = sin_rows.astype(jnp.bfloat16)
                    return carry
                lax.fori_loop(0, width // FINE, one, 0)

    exchange = [
        remote(moved.at[1, t], gx.at[t, 1, 0, 0], ex_s.at[t], ex_r.at[t], slots - 1 - g, a)
        for t in range(chunks)
    ]
    edges = [
        remote(top, eg.at[c, m], eg_s.at[c, m], eg_r.at[c, m],
               across, 2 * ((q + chips - m) % chips) + (core + c) % 2)
        for c in range(2) for m in range(chips)
    ]

    def mine(t, s):
        return gx.at[t, 1, 0, 0] if s else moved.at[0, t]

    def over_chips(t, s, m):
        return remote(mine(t, s), gx.at[t, s, 0, m], x_s.at[t, s, m], x_r.at[t, s, m],
                      g, 2 * ((q + chips - m) % chips) + core)

    def over_cores(t, s, m):
        source = gx.at[t, s, 0, m] if m else mine(t, s)
        return remote(source, gx.at[t, s, 1, m], c_s.at[t, s, m], c_r.at[t, s, m], g, partner)

    def to_grid(t, d):
        to = (g + d) % slots
        return remote(half.at[t, to], arr.at[t, g], a_s.at[t, d], a_r.at[t, d], to, a)

    exchange[0].start()

    @pl.when(high)
    def _():
        for copy in edges:
            copy.start()
        eg[...] = jnp.zeros_like(eg)

    for t in range(1, chunks):
        exchange[t].start()
    for t in range(chunks):
        for m in range(1, chips):
            over_chips(t, 0, m).start()
        over_cores(t, 0, 0).start()
    bring.start()
    build_factors(0)
    build_tables()
    for t in range(chunks):
        for m in range(1, chips):
            over_chips(t, 0, m).wait_recv()
            over_cores(t, 0, m).start()
    def spread(t):
        exchange[t].wait_recv()
        for m in range(1, chips):
            over_chips(t, 1, m).start()
        over_cores(t, 1, 0).start()

    spread(0)
    for t in range(chunks):
        for m in range(1, chips):
            over_chips(t, 1, m).wait_recv()
            over_cores(t, 1, m).start()
        if t + 1 < chunks:
            spread(t + 1)
        if t == 0:
            @pl.when(low)
            def _():
                for copy in edges:
                    copy.wait_recv()
        for s in range(2):
            for m in range(chips):
                over_cores(t, s, m).wait_recv()
        own_pair = column(info, t, 2) > 0.5
        sign = column(info, t, 3)
        for j in range(2 * chips):
            c, m = divmod(j, chips)
            span = slice(j * width, (j + 1) * width)
            turned_rows = []
            for s in range(2):
                source = moved.at[0, t] if s + j == 0 else gx.at[t, s, c, m]
                fields = [[source[f, i].astype(jnp.float32) for i in range(2)] for f in range(3)]
                if s == 1 and t == 0:
                    put = column(info, t, 4)[:EDGE] > 0.5
                    for f in range(3):
                        for i in range(2):
                            top = jnp.where(put, eg[c, m, f, i].astype(jnp.float32), fields[f][i][:EDGE])
                            fields[f][i] = (
                                jnp.concatenate([top, fields[f][i][EDGE:]], axis=0) if hb > EDGE else top
                            )
                turned_rows.append(wave_exponential(
                    fields, column(info, t, s), ky[:, span], (sine[t, s, :, span], cosine[t, s, :, span])
                ))
            for f in range(3):
                (re0, im0), (re1, im1) = turned_rows[0][f], turned_rows[1][f]
                for i, value in enumerate((
                    jnp.where(own_pair, re0, re0 + re1), jnp.where(own_pair, re1, sign * (im0 - im1))
                )):
                    rows_c[(i * 3 + f) * hb : (i * 3 + f + 1) * hb, span] = value.astype(jnp.bfloat16)
                for i, value in enumerate((
                    jnp.where(own_pair, -im0, -(im0 + im1)), jnp.where(own_pair, -im1, sign * (re0 - re1))
                )):
                    rows_s[(i * 3 + f) * hb : (i * 3 + f + 1) * hb, span] = value.astype(jnp.bfloat16)
        tile = min(length, max(block, 256))
        for y in range(0, length, tile):
            value = (
                jnp.dot(rows_c[...], ct[:, y : y + tile], preferred_element_type=jnp.float32)
                + jnp.dot(rows_s[...], st[:, y : y + tile], preferred_element_type=jnp.float32)
            ).astype(jnp.bfloat16)
            for b in range(tile // block):
                for i in range(2):
                    for f in range(3):
                        half[t, y // block + b, i * hb : (i + 1) * hb, f * block : (f + 1) * block] = (
                            value[(i * 3 + f) * hb : (i * 3 + f + 1) * hb, b * block : (b + 1) * block]
                        )
        for d in sending(slots):
            to_grid(t, d).start()
        pltpu.make_async_copy(half.at[t, g], arr.at[t, g], l_s.at[t]).start()
    def to_rows(t, d):
        to = (g + d) % slots
        return remote(fh.at[t, to], ret.at[t, g], b_s.at[t, d], b_r.at[t, d], to, a)

    def sum_cores(t):
        return remote(stage.at[t, 1], rsin.at[t], d_s.at[t], d_r.at[t], g, partner)

    def sum_chips(t, m):
        return remote(xs.at[t, m], rx.at[t, m], y_s.at[t, m], y_r.at[t, m],
                      g, 2 * ((q + m) % chips) + core)

    def give(t):
        return remote(fin.at[t], other.at[t], gv_s.at[t], gv_r.at[t], slots - 1 - g, a)

    last = remote(fin.at[0, :, :, :EDGE], edge, le_s, le_r, edge_partner(g, slots), a)

    bring.wait()
    for t in range(chunks):
        for d in range(1, slots):
            to_grid(t, d).wait_recv()
        pltpu.make_async_copy(half.at[t, g], arr.at[t, g], l_s.at[t]).wait()
        together = max(1, 128 // (2 * hb))
        for p in range(0, slots, together):
            value = arr[t, p : p + together].astype(jnp.float32)
            value = value.reshape(together * 2 * hb, 3 * block)
            spot = p * 2 * hb
            arr_t[:, spot : spot + together * 2 * hb] = value.T.astype(jnp.bfloat16)
        depth = length // chunks
        for x in range(0, length, 256):
            value = jnp.dot(
                arr_t[...], packed[t * depth : (t + 1) * depth, x : x + 256],
                preferred_element_type=jnp.float32,
            )
            if t:
                value = value + grid[:, x : x + 256]
            if t < chunks - 1:
                grid[:, x : x + 256] = value
            else:
                value = value * (1.0 / length)
                east, north, height = (value[i * block : (i + 1) * block] for i in range(3))
                for k, pair in enumerate((
                    east * east, east * north, north * north, east * height, north * height
                )):
                    products[k * block : (k + 1) * block, x : x + 256] = pair.astype(jnp.bfloat16)
    for t in range(chunks):
        for k in range(0, depth, 256):
            value = lax.dot_general(
                packed[t * depth + k : t * depth + k + 256, :], products[...], DIMS_NT,
                preferred_element_type=jnp.float32,
            ).astype(jnp.bfloat16)
            for n in range(256 // (2 * hb)):
                fh[t, k // (2 * hb) + n] = value[n * 2 * hb : (n + 1) * 2 * hb]
        for d in sending(slots):
            to_rows(t, d).start()
        pltpu.make_async_copy(fh.at[t, g], ret.at[t, g], m_s.at[t]).start()
    own_factors()

    @pl.when(low)
    def _():
        edge[...] = jnp.zeros_like(edge)

    def finish(t):
        for m in range(1, chips):
            sum_chips(t, m).wait_recv()
            acc[...] += rx[t, m].astype(jnp.float32)
        fin[t] = acc[1].astype(jnp.bfloat16)
        give(t).start()
        if t == 0:
            @pl.when(low)
            def _():
                last.start()
        own[t] = acc[0].astype(jnp.bfloat16)

    for t in range(chunks):
        for d in range(1, slots):
            to_rows(t, d).wait_recv()
        pltpu.make_async_copy(fh.at[t, g], ret.at[t, g], m_s.at[t]).wait()
        for p in range(slots):
            for k in range(5):
                lhs[k * 2 * hb : (k + 1) * 2 * hb, p * block : (p + 1) * block] = (
                    ret[t, p, :, k * block : (k + 1) * block]
                )
        own_pair = column(info, t, 2) > 0.5
        sign, scale = column(info, t, 3), column(info, t, 5)
        for j in range(2 * chips):
            c, m = divmod(j, chips)
            span = slice(j * width, (j + 1) * width)
            by_c = lax.dot_general(lhs[...], ct[span, :], DIMS_NT, preferred_element_type=jnp.float32)
            by_s = lax.dot_general(lhs[...], st[span, :], DIMS_NT, preferred_element_type=jnp.float32)

            def part(values, k, i):
                return values[(2 * k + i) * hb : (2 * k + i + 1) * hb]

            for s in range(2):
                turn = scale * sign if s == 0 else -scale * sign
                real, imag = [], []
                for k in range(5):
                    rc, ic = part(by_c, k, 0), part(by_c, k, 1)
                    rs, iz = part(by_s, k, 0), part(by_s, k, 1)
                    real.append(jnp.where(own_pair, scale * (ic if s else rc), scale * rc + turn * iz))
                    imag.append(jnp.where(own_pair, -scale * (iz if s else rs), turn * ic - scale * rs))
                kx, kyj = column(info, t, s), ky[:, span]
                tendency = [
                    (kx * imag[u] + kyj * imag[v], -(kx * real[u] + kyj * real[v]))
                    for u, v in ((0, 1), (1, 2), (3, 4))
                ]
                back = wave_exponential(
                    tendency, kx, kyj, (-sine[t, s, :, span], cosine[t, s, :, span])
                )
                for f in range(3):
                    for i in range(2):
                        stage[t, c, m, s, f, i] = back[f][i].astype(jnp.bfloat16)
        sum_cores(t).start()
        if t:
            finish(t - 1)
        sum_cores(t).wait_recv()
        for m in range(1, chips):
            xs[t, m] = (
                stage[t, 0, m].astype(jnp.float32) + rsin[t, m].astype(jnp.float32)
            ).astype(jnp.bfloat16)
            sum_chips(t, m).start()
        acc[...] = stage[t, 0, 0].astype(jnp.float32) + rsin[t, 0].astype(jnp.float32)
    finish(chunks - 1)
    for t in range(chunks):
        give(t).wait_recv()

    @pl.when(high)
    def _():
        last.wait_recv()

    for t in range(chunks):
        exchange[t].wait_send()
        for s in range(2):
            for m in range(1, chips):
                over_chips(t, s, m).wait_send()
            for m in range(chips):
                over_cores(t, s, m).wait_send()
        for d in range(1, slots):
            to_grid(t, d).wait_send()

    @pl.when(high)
    def _():
        for copy in edges:
            copy.wait_send()


    for t in range(chunks):
        for d in range(1, slots):
            to_rows(t, d).wait_send()
        sum_cores(t).wait_send()
        for m in range(1, chips):
            sum_chips(t, m).wait_send()
        give(t).wait_send()

    @pl.when(low)
    def _():
        last.wait_send()


    for f in range(3):
        for i in range(2):
            rows = jnp.concatenate(
                [own[t, f, i] for t in range(chunks)] + [other[t, f, i] for t in range(chunks)]
                + [edge[f, i]], axis=0,
            )
            averaged = jnp.dot(back_rows[side], rows, preferred_element_type=jnp.float32)
            result[f, i] = state[f, i] + time_step * averaged
    fields = [[result[f, i] for i in range(2)] for f in range(3)]
    advanced = wave_exponential(fields, own_kx[...], ky[:, :width], (end_sine[...], end_cosine[...]))
    for f in range(3):
        for i in range(2):
            result[f, i] = advanced[f][i]


VMEM = pl.BlockSpec(memory_space=pltpu.VMEM)


def per_device(spectral_state, phase_index, weight_count):
    slots, owners = lax.axis_size("space"), lax.axis_size("avg")
    block, width = spectral_state.shape[2:]
    length, half = block * slots, block // 2
    chips = owners // 2
    chunks = max(1, half // CHUNK_ROWS)
    hb = half // chunks
    dims = (slots, chips, chunks, hb, width, block)
    g, a = lax.axis_index("space"), lax.axis_index("avg")
    q, core = a // 2, a % 2
    low = g < slots // 2
    phase = phase_index[0].astype(jnp.float32) * phase_step
    weight = weight_count[0].astype(jnp.float32) / (weight_scale * owners)

    m, c = jnp.arange(chips, dtype=jnp.int32), jnp.arange(2, dtype=jnp.int32)[:, None]
    order = (2 * ((q + m) % chips) + (core + c) % 2).reshape(-1)
    columns = (order[:, None] * width + jnp.arange(width, dtype=jnp.int32)).reshape(1, -1)
    ky = wave_of(columns, length)
    packed = jnp.asarray(packed_table(length, slots, chunks))

    base = jnp.where(low, 2 * half * g, 2 * half * (slots - 1 - g) + half)
    direct = base + jnp.arange(half, dtype=jnp.int32)
    mirror = jnp.where(direct == 0, length // 2, length - direct)
    first = wave_of(jnp.where(low, direct, mirror), length)
    second = wave_of(jnp.where(low, mirror, direct), length)
    ones = jnp.ones((half,), jnp.float32)
    start = (jnp.arange(half) == 0) & low
    info = jnp.stack([
        first, second, (direct == 0).astype(jnp.float32), jnp.where(low, ones, -ones),
        start.astype(jnp.float32), ones * (weight / length), ones, ones,
    ], axis=1).reshape(chunks, hb, 8)
    own_kx = wave_of(g * block + jnp.arange(block, dtype=jnp.int32)[:, None], length)

    r = np.arange(half)
    into = np.zeros((2, 2, half, block), np.float32)
    into[0, 0, r, r] = 1
    into[0, 1, r, half + r] = 1
    into[1, 0, r, half - r] = 1
    into[1, 1, r[1:], block - r[1:]] = 1
    into = jnp.asarray(into.reshape(2, block, block).astype(ml_dtypes.bfloat16))
    back = np.zeros((2, block, 2 * half + EDGE), np.float32)
    back[0, r, r] = 1
    back[0, half + r, half + r] = 1
    back[1, half - r, r] = 1
    back[1, block - r[1:], half + r[1:]] = 1
    back[1, 0, 2 * half] = 1
    back = jnp.asarray(back.astype(ml_dtypes.bfloat16))

    piece = (3, 2, hb, width)
    dma = pltpu.SemaphoreType.DMA
    vmem = lambda *shape: pltpu.VMEM(shape, jnp.bfloat16)
    wide = lambda *shape: pltpu.VMEM(shape, jnp.float32)
    return pl.pallas_call(
        functools.partial(step_kernel, dims),
        out_shape=jax.ShapeDtypeStruct(spectral_state.shape, jnp.float32),
        in_specs=[VMEM] * 10 + [pl.BlockSpec(memory_space=pl.ANY)],
        out_specs=VMEM,
        scratch_shapes=[
            vmem(2, chunks, *piece), vmem(3, 2, EDGE, width),
            vmem(chunks, 2, 2, chips, *piece), vmem(2, chips, 3, 2, EDGE, width),
            vmem(6 * hb, length), vmem(6 * hb, length),
            vmem(chunks, slots, 2 * hb, 3 * block), vmem(chunks, slots, 2 * hb, 3 * block),
            vmem(3 * block, length // chunks), wide(3 * block, length), vmem(5 * block, length),
            vmem(length, length), vmem(length, length), vmem(length, length),
            wide(chunks, 2, hb, length), wide(chunks, 2, hb, length),
            wide(block, width), wide(block, width),
            vmem(chunks, slots, 2 * hb, 5 * block), vmem(chunks, slots, 2 * hb, 5 * block),
            vmem(10 * hb, length),
            vmem(chunks, 2, chips, 2, *piece), vmem(chunks, chips, 2, *piece),
            wide(2, *piece), vmem(chunks, chips, 2, *piece), vmem(chunks, chips, 2, *piece),
            vmem(chunks, *piece), vmem(chunks, *piece), vmem(chunks, *piece),
            vmem(3, 2, EDGE, width),
            dma((chunks,)), dma((chunks,)),
            dma((2, chips)), dma((2, chips)),
            dma((chunks, 2, chips)), dma((chunks, 2, chips)),
            dma((chunks, 2, chips)), dma((chunks, 2, chips)),
            dma((chunks, slots)), dma((chunks, slots)), dma((chunks,)),
            dma((chunks, slots)), dma((chunks, slots)), dma((chunks,)),
            dma((chunks,)), dma((chunks,)),
            dma((chunks, chips)), dma((chunks, chips)),
            dma((chunks,)), dma((chunks,)),
            dma(()), dma(()), dma(()),
        ],
        compiler_params=pltpu.CompilerParams(
            collective_id=0, has_side_effects=True, vmem_limit_bytes=56 * 2**20
        ),
        name="averaged_step",
    )(spectral_state, into, back, info, ky, own_kx, phase.reshape(1, 1),
      *angle_tables(length, width, owners), packed)


def signal_all(barrier, peers):
    for space, avg in peers:
        pl.semaphore_signal(
            barrier, inc=1, device_id={"space": space, "avg": avg}, device_id_type=MESH
        )


def only_row(n, value, rows):
    spot = lax.broadcasted_iota(jnp.int32, (rows, value.shape[-1]), 0)
    return jnp.where(spot == n, jnp.broadcast_to(value, (rows, value.shape[-1])), 0.0)


def cube_kernel(
    dims, phase_ref, weight_ref, state_hbm, table_hbm, result,
    state, order_rows, info, ky, own_kx, parts, ph_mine, ph_got, moved, top, gx, eg, rows_c, rows_s, half, arr, arr_t, grid, products, packed,
    ct, st, sine, cosine, end_sine, end_cosine, fh, ret, lhs, stage, rsin, xs, rb, lt, le,
    ph_s, ph_r, x_s, x_r, c_s, c_r, g_s, eg_s, eg_r, a_s, a_r, l_s,
    b_s, b_r, m_s, d_s, d_r, y_s, y_r, k_s, le_s, le_r, load_s,
):
    slots, chunks, hb, width, block = dims
    length, reach = slots * block, block // 2
    g, a, q, core = positions()
    side = g // (slots // 2)
    pair_block = g + side * (slots - 1 - 2 * g)
    me = 2 * pair_block + q
    mirror = slots - 1 - g
    partner = 2 * q + 1 - core
    low, high = side == 0, side == 1

    def place(slot):
        b = slot // 2
        return b + side * (slots - 1 - 2 * b), 2 * (slot % 2) + core

    def chip(m):
        return (q + m) % 2

    barrier = pltpu.get_barrier_semaphore()
    near = [place((me + d) % slots) for d in range(1, slots)] + [(g, partner)]
    near += [(mirror, 2 * chip(m) + core) for m in range(2)]
    across = edge_partner(g, slots)
    below = [(across, c) for c in range(2)] + [(slots - 1 - across, c) for c in range(2)]
    source = edge_partner(pair_block, slots)
    above = [(source, c) for c in range(4)]
    signal_all(barrier, near)

    @pl.when(high)
    def _():
        signal_all(barrier, below)

    @pl.when(q == 0)
    def _():
        signal_all(barrier, above)
    loads = [
        pltpu.make_async_copy(source_ref, target, load_s.at[n])
        for n, (source_ref, target) in enumerate((
            (state_hbm, state), (table_hbm, parts)
        ))
    ]
    for copy in loads:
        copy.start()

    def wave(spot):
        return jnp.where(spot >= length // 2, spot - length, spot).astype(jnp.float32) * (2.0 / length)

    lane = lax.broadcasted_iota(jnp.int32, (hb, 128), 1)
    for t in range(chunks):
        spot = lax.broadcasted_iota(jnp.int32, (hb, 128), 0) + t * hb
        direct = spot + (block * pair_block + reach * q)
        mirrored = jnp.where(direct == 0, length // 2, length - direct)
        begins = jnp.where(spot == 0, 1.0, 0.0)
        info[t] = jnp.where(lane == 0, wave(direct), jnp.where(lane == 1, wave(mirrored), jnp.where(
            lane == 2, jnp.where(direct == 0, 1.0, 0.0), jnp.where(
                lane == 3, begins * (1 - q).astype(jnp.float32), begins * side.astype(jnp.float32)
            )
        )))
    own_kx[...] = wave(lax.broadcasted_iota(jnp.int32, (block, 128), 0) + g * block)
    for j in range(4):
        c, m = divmod(j, 2)
        owner = 2 * ((q + m) % 2) + (core + c) % 2
        spot = lax.broadcasted_iota(jnp.int32, (1, width), 1) + owner * width
        ky[:, j * width : (j + 1) * width] = wave(spot)
    down = lax.broadcasted_iota(jnp.int32, (block, block), 0)
    along = lax.broadcasted_iota(jnp.int32, (block, block), 1)
    turned_down = jnp.where(down == 0, 0, block - down)
    order_rows[...] = jnp.where(
        along == down + side * (turned_down - down), 1.0, 0.0
    ).astype(jnp.bfloat16)
    lane = lax.broadcasted_iota(jnp.int32, ph_mine.shape, 1)
    ph_mine[...] = jnp.where(
        lane == 0, phase_ref[0].astype(jnp.float32) * phase_step,
        weight_ref[0].astype(jnp.float32) / (weight_scale * 4),
    )
    loads[0].wait()

    top_tile = jnp.zeros((EDGE, width), jnp.float32)
    for f in range(3):
        for i in range(2):
            plane = state[f, i].astype(jnp.bfloat16)
            top_tile = top_tile + only_row(2 * f + i, state[f, i, 0:1, :], EDGE)
            picked = jnp.dot(order_rows[...], plane, preferred_element_type=jnp.float32)
            picked = picked.astype(jnp.bfloat16)
            for h in range(2):
                for t in range(chunks):
                    spot = h * reach + t * hb
                    moved[h, t, f, i] = picked[spot : spot + hb]
    top[...] = top_tile.astype(jnp.bfloat16)
    pl.semaphore_wait(barrier, len(near) + len(below) * side + len(above) * (1 - q))

    def build_factors(t):
        turn = chosen_phase()[:, 0:1]
        if True:
            for s in range(2):
                def one(j, carry, t=t, s=s):
                    span = pl.ds(pl.multiple_of(j * 256, 256), 256)
                    factors = wave_factors(column(info, t, s), ky[:, span], turn)
                    sine[t, s, :, span], cosine[t, s, :, span] = factors
                    return carry
                lax.fori_loop(0, length // 256, one, 0)

    def chosen_phase():
        keep = 1.0 - jnp.abs(q - side).astype(jnp.float32)
        return ph_got[0:1] + keep * (ph_mine[0:1] - ph_got[0:1])

    steps, owners = width // FINE, 4

    def begin_rows(owner, h):
        return turned(
            (parts[pl.ds(2 * (FINE + steps) + owner, 1)], parts[pl.ds(2 * (FINE + steps) + owners + owner, 1)]),
            (parts[pl.ds(2 * FINE + h, 1)], parts[pl.ds(2 * FINE + steps + h, 1)]),
        )

    def fine_rows(begin):
        return turned(begin, (parts[0:FINE], parts[FINE : 2 * FINE]))

    def build_packed():
        def one(n, carry):
            begin = begin_rows(n // steps, n % steps)
            cos_rows, sin_rows = fine_rows(begin)
            slot, t = n // chunks, n % chunks
            at = pl.multiple_of((t * slots + slot) * 2 * hb, 2 * hb)
            packed[pl.ds(at, hb), :] = cos_rows.astype(jnp.bfloat16)
            packed[pl.ds(at + hb, hb), :] = (-sin_rows).astype(jnp.bfloat16)
            return carry
        lax.fori_loop(0, length // (2 * FINE), one, 0)
        down = lax.broadcasted_iota(jnp.int32, (hb, length), 0)
        along = lax.broadcasted_iota(jnp.int32, (hb, length), 1)
        rest = packed[hb : 2 * hb, :].astype(jnp.float32)
        packed[hb : 2 * hb, :] = jnp.where(
            down == 0, 1.0 - 2.0 * (along % 2).astype(jnp.float32), rest
        ).astype(jnp.bfloat16)

    def build_tables():
        for c in range(2):
            for m in range(2):
                owner = 2 * chip(m) + (core + c) % 2

                def one(h, carry, j=c * 2 + m, owner=owner):
                    cos_rows, sin_rows = fine_rows(begin_rows(owner, h))
                    at = pl.ds(pl.multiple_of(j * width + h * FINE, FINE), FINE)
                    ct[at, :] = cos_rows.astype(jnp.bfloat16)
                    st[at, :] = sin_rows.astype(jnp.bfloat16)
                    return carry
                lax.fori_loop(0, width // FINE, one, 0)

    swap_phase = remote(ph_mine, ph_got, ph_s, ph_r, g, 2 * chip(1) + core)

    def bring_own(t):
        return remote(moved.at[chip(1), t], gx.at[t, side, 0, 1], x_s.at[t, 0], x_r.at[t, 0],
                      g, 2 * chip(1) + core)

    def bring_mirror(t, m):
        return remote(moved.at[chip(m), t], gx.at[t, side, 0, m], x_s.at[t, 1 + m], x_r.at[t, 1 + m],
                      mirror, 2 * chip(m) + core)

    def keep_own(t):
        return pltpu.make_async_copy(moved.at[q, t], gx.at[t, side, 0, 0], g_s.at[t])

    def over_cores(t, kind, m):
        role = (1 - side) if kind else side
        piece = gx.at[t, role, 0, m] if kind + m else moved.at[q, t]
        return remote(piece, gx.at[t, role, 1, m], c_s.at[t, kind, m], c_r.at[t, kind, m], g, partner)

    edges = [
        remote(top, eg.at[c, q], eg_s.at[k, c], eg_r.at[c, q], space, (core + c) % 2)
        for k, space in enumerate((across, slots - 1 - across)) for c in range(2)
    ]

    def to_grid(t, d):
        to = (me + d) % slots
        space, avg = place(to)
        return remote(half.at[t, to], arr.at[t, me], a_s.at[t, d], a_r.at[t, d], space, avg)

    def to_rows(t, d):
        to = (me + d) % slots
        space, avg = place(to)
        return remote(fh.at[t, to], ret.at[t, me], b_s.at[t, d], b_r.at[t, d], space, avg)

    def sum_cores(t):
        return remote(stage.at[t, 1], rsin.at[t], d_s.at[t], d_r.at[t], g, partner)

    def give_own(t):
        return remote(xs.at[t, 1, side], rb.at[t, 0, q], y_s.at[t, 0], y_r.at[t, 0],
                      g, 2 * chip(1) + core)

    def give_mirror(t, m):
        return remote(xs.at[t, m, 1 - side], rb.at[t, 1, q], y_s.at[t, 1 + m], y_r.at[t, 1 + m],
                      mirror, 2 * chip(m) + core)

    def give_self(t):
        return pltpu.make_async_copy(xs.at[t, 0, side], rb.at[t, 0, q], k_s.at[t])

    last = [
        remote(lt.at[m], le.at[side], le_s.at[m], le_r.at[side], source, 2 * chip(m) + core)
        for m in range(2)
    ]

    swap_phase.start()

    @pl.when(high)
    def _():
        for copy in edges:
            copy.start()
    def launch(t):
        for m in range(2):
            bring_mirror(t, m).start()
        bring_own(t).start()
        over_cores(t, 0, 0).start()
        keep_own(t).start()

    launch(0)
    pass
    @pl.when(q != 0)
    def _():
        eg[...] = jnp.zeros_like(eg)

    @pl.when(low)
    def _():
        le[...] = jnp.zeros_like(le)
    swap_phase.wait_recv()
    scale = chosen_phase()[:, 1:2] * (1.0 / length)

    def meet_edges():
        @pl.when(q == 0)
        def _():
            for c in range(2):
                for m in range(2):
                    remote(top, eg.at[c, m], eg_s.at[0, c], eg_r.at[c, m], g, partner).wait_recv()

    def rotate(t):
        bring_own(t).wait_recv()
        over_cores(t, 0, 1).start()
        for m in range(2):
            bring_mirror(t, m).wait_recv()
            over_cores(t, 1, m).start()
        keep_own(t).wait()
        for kind in range(2):
            for m in range(2):
                over_cores(t, kind, m).wait_recv()
        own_pair = column(info, t, 2) > 0.5
        for j in range(4):
            c, m = divmod(j, 2)
            span = slice(j * width, (j + 1) * width)
            turned_rows = []
            for s in range(2):
                piece = gx.at[t, s, c, m]
                fields = [[piece[f, i].astype(jnp.float32) for i in range(2)] for f in range(3)]
                if s == 1 and t == 0:
                    put = column(info, t, 3) > 0.5
                    tile = eg[c, m].astype(jnp.float32)
                    for f in range(3):
                        for i in range(2):
                            n = 2 * f + i
                            row = jnp.broadcast_to(tile[n : n + 1], (hb, width))
                            fields[f][i] = jnp.where(put, row, fields[f][i])
                turned_rows.append(wave_exponential(
                    fields, column(info, t, s), ky[:, span], (sine[t, s, :, span], cosine[t, s, :, span])
                ))
            for f in range(3):
                (re0, im0), (re1, im1) = turned_rows[0][f], turned_rows[1][f]
                for i, value in enumerate((
                    jnp.where(own_pair, re0, re0 + re1), jnp.where(own_pair, re1, im0 - im1)
                )):
                    rows_c[(i * 3 + f) * hb : (i * 3 + f + 1) * hb, span] = value.astype(jnp.bfloat16)
                for i, value in enumerate((
                    jnp.where(own_pair, -im0, -(im0 + im1)), jnp.where(own_pair, -im1, re0 - re1)
                )):
                    rows_s[(i * 3 + f) * hb : (i * 3 + f + 1) * hb, span] = value.astype(jnp.bfloat16)
        tile = min(length, max(block, 256))
        for y in range(0, length, tile):
            value = (
                jnp.dot(rows_c[...], ct[:, y : y + tile], preferred_element_type=jnp.float32)
                + jnp.dot(rows_s[...], st[:, y : y + tile], preferred_element_type=jnp.float32)
            ).astype(jnp.bfloat16)
            for b in range(tile // block):
                for i in range(2):
                    for f in range(3):
                        half[t, y // block + b, i * hb : (i + 1) * hb, f * block : (f + 1) * block] = (
                            value[(i * 3 + f) * hb : (i * 3 + f + 1) * hb, b * block : (b + 1) * block]
                        )
        for d in sending(slots):
            to_grid(t, d).start()
        pltpu.make_async_copy(half.at[t, me], arr.at[t, me], l_s.at[t]).start()

    depth = length // chunks

    def on_grid(t):
        for d in range(1, slots):
            to_grid(t, d).wait_recv()
        pltpu.make_async_copy(half.at[t, me], arr.at[t, me], l_s.at[t]).wait()
        together = max(1, 128 // (2 * hb))
        for p in range(0, slots, together):
            value = arr[t, p : p + together].astype(jnp.float32)
            value = value.reshape(together * 2 * hb, 3 * block)
            spot = p * 2 * hb
            arr_t[:, spot : spot + together * 2 * hb] = value.T.astype(jnp.bfloat16)
        for x in range(0, length, 256):
            value = jnp.dot(
                arr_t[...], packed[t * depth : (t + 1) * depth, x : x + 256],
                preferred_element_type=jnp.float32,
            )
            if t:
                value = value + grid[:, x : x + 256]
            if t < chunks - 1:
                grid[:, x : x + 256] = value
            else:
                value = value * (1.0 / length)
                east, north, height = (value[i * block : (i + 1) * block] for i in range(3))
                for k, pair in enumerate((
                    east * east, east * north, north * north, east * height, north * height
                )):
                    products[k * block : (k + 1) * block, x : x + 256] = pair.astype(jnp.bfloat16)

    loads[1].wait()
    build_tables()
    build_factors(0)
    launch(1)
    build_factors(1)
    meet_edges()
    rotate(0)
    launch(2)
    build_packed()
    build_factors(2)
    rotate(1)
    launch(3)
    on_grid(0)
    build_factors(3)
    rotate(2)
    on_grid(1)
    rotate(3)
    on_grid(2)
    end_sine[...], end_cosine[...] = wave_factors(own_kx[:, 0:1], ky[:, :width], time_step)
    on_grid(chunks - 1)

    for t in range(chunks):
        for k in range(0, depth, 256):
            value = lax.dot_general(
                packed[t * depth + k : t * depth + k + 256, :], products[...], DIMS_NT,
                preferred_element_type=jnp.float32,
            ).astype(jnp.bfloat16)
            for n in range(256 // (2 * hb)):
                fh[t, k // (2 * hb) + n] = value[n * 2 * hb : (n + 1) * 2 * hb]
        for d in sending(slots):
            to_rows(t, d).start()
        pltpu.make_async_copy(fh.at[t, me], ret.at[t, me], m_s.at[t]).start()

    def pass_on(t):
        sum_cores(t).wait_recv()
        for m in range(2):
            for s in range(2):
                value = stage[t, 0, m, s].astype(jnp.float32) + rsin[t, m, s].astype(jnp.float32)
                xs[t, m, s] = value.astype(jnp.bfloat16)
                if t == 0 and s == 1:
                    tile = jnp.zeros((EDGE, width), jnp.float32)
                    for f in range(3):
                        for i in range(2):
                            tile = tile + only_row(2 * f + i, value[f, i, 0:1], EDGE)
                    lt[m] = tile.astype(jnp.bfloat16)
        for m in range(2):
            give_mirror(t, m).start()
        give_own(t).start()
        give_self(t).start()
        if t == 0:
            @pl.when(q == 0)
            def _():
                for copy in last:
                    copy.start()

    for t in range(chunks):
        for d in range(1, slots):
            to_rows(t, d).wait_recv()
        pltpu.make_async_copy(fh.at[t, me], ret.at[t, me], m_s.at[t]).wait()
        for p in range(slots):
            for k in range(5):
                lhs[k * 2 * hb : (k + 1) * 2 * hb, p * block : (p + 1) * block] = (
                    ret[t, p, :, k * block : (k + 1) * block]
                )
        own_pair = column(info, t, 2) > 0.5
        for j in range(4):
            c, m = divmod(j, 2)
            span = slice(j * width, (j + 1) * width)
            by_c = lax.dot_general(lhs[...], ct[span, :], DIMS_NT, preferred_element_type=jnp.float32)
            by_s = lax.dot_general(lhs[...], st[span, :], DIMS_NT, preferred_element_type=jnp.float32)

            def part(values, k, i):
                return values[(2 * k + i) * hb : (2 * k + i + 1) * hb] * scale

            for s in range(2):
                real, imag = [], []
                for k in range(5):
                    rc, ic = part(by_c, k, 0), part(by_c, k, 1)
                    rs, iz = part(by_s, k, 0), part(by_s, k, 1)
                    real.append(jnp.where(own_pair, (ic if s else rc), (rc - iz if s else rc + iz)))
                    imag.append(jnp.where(own_pair, -(iz if s else rs), (-ic if s else ic) - rs))
                kx, kyj = column(info, t, s), ky[:, span]
                tendency = [
                    (kx * imag[u] + kyj * imag[v], -(kx * real[u] + kyj * real[v]))
                    for u, v in ((0, 1), (1, 2), (3, 4))
                ]
                back = wave_exponential(
                    tendency, kx, kyj, (-sine[t, s, :, span], cosine[t, s, :, span])
                )
                for f in range(3):
                    for i in range(2):
                        stage[t, c, m, s, f, i] = back[f][i].astype(jnp.bfloat16)
        sum_cores(t).start()
        pass_on(t)

    for t in range(chunks):
        bring_own(t).wait_send()
        for m in range(2):
            bring_mirror(t, m).wait_send()
        for kind in range(2):
            for m in range(2):
                over_cores(t, kind, m).wait_send()
        for d in range(1, slots):
            to_grid(t, d).wait_send()
            to_rows(t, d).wait_send()
        sum_cores(t).wait_send()
    swap_phase.wait_send()

    @pl.when(high)
    def _():
        for copy in edges:
            copy.wait_send()
        for k in range(2):
            remote(lt.at[0], le.at[k], le_s.at[0], le_r.at[k], g, partner).wait_recv()

    for t in range(chunks):
        give_own(t).wait_recv()
        for m in range(2):
            give_mirror(t, m).wait_recv()
        give_self(t).wait()

    edge = le[0].astype(jnp.float32) + le[1].astype(jnp.float32)
    for f in range(3):
        for i in range(2):
            pieces = [
                rb[t, 0, h, f, i].astype(jnp.float32) + rb[t, 1, h, f, i].astype(jnp.float32)
                for h in range(2) for t in range(chunks)
            ]
            n = 2 * f + i
            pieces[0] = jnp.where(
                column(info, 0, 4) > 0.5, jnp.broadcast_to(edge[n : n + 1], (hb, width)), pieces[0]
            )
            rows = jnp.concatenate(pieces, axis=0).astype(jnp.bfloat16)
            averaged = jnp.dot(order_rows[...], rows, preferred_element_type=jnp.float32)
            result[f, i] = state[f, i] + time_step * averaged
    fields = [[result[f, i] for i in range(2)] for f in range(3)]
    advanced = wave_exponential(fields, own_kx[:, 0:1], ky[:, :width], (end_sine[...], end_cosine[...]))
    for f in range(3):
        for i in range(2):
            result[f, i] = advanced[f][i] - state[f, i]

    for t in range(chunks):
        give_own(t).wait_send()
        for m in range(2):
            give_mirror(t, m).wait_send()

    @pl.when(q == 0)
    def _():
        for copy in last:
            copy.wait_send()


def cube_step(spectral_state, phase_index, weight_count):
    slots, owners = lax.axis_size("space"), lax.axis_size("avg")
    block, width = spectral_state.shape[2:]
    length, half = block * slots, block // 2
    chunks = max(1, half // CHUNK_ROWS)
    hb = half // chunks
    dims = (slots, chunks, hb, width, block)
    spans = ((1, FINE), (FINE, width // FINE), (width, owners))
    table = np.concatenate([
        part for step, count in spans
        for part in circle(step * np.arange(count)[:, None] * np.arange(length), length)
    ])
    table = jnp.asarray(table)
    piece = (3, 2, hb, width)
    dma = pltpu.SemaphoreType.DMA
    vmem = lambda *shape: pltpu.VMEM(shape, jnp.bfloat16)
    wide = lambda *shape: pltpu.VMEM(shape, jnp.float32)
    return spectral_state + pl.pallas_call(
        functools.partial(cube_kernel, dims),
        out_shape=jax.ShapeDtypeStruct(spectral_state.shape, jnp.float32),
        in_specs=[pl.BlockSpec(memory_space=pltpu.SMEM)] * 2 + [pl.BlockSpec(memory_space=pl.ANY)] * 2,
        out_specs=VMEM,
        scratch_shapes=[
            wide(3, 2, block, width), vmem(block, block), wide(chunks, hb, 128), wide(1, length),
            wide(block, 128), wide(*table.shape),
            wide(8, 128), wide(8, 128),
            vmem(2, chunks, *piece), vmem(EDGE, width),
            vmem(chunks, 2, 2, 2, *piece), vmem(2, 2, EDGE, width),
            vmem(6 * hb, length), vmem(6 * hb, length),
            vmem(chunks, slots, 2 * hb, 3 * block), vmem(chunks, slots, 2 * hb, 3 * block),
            vmem(3 * block, length // chunks), wide(3 * block, length), vmem(5 * block, length),
            vmem(length, length), vmem(length, length), vmem(length, length),
            wide(chunks, 2, hb, length), wide(chunks, 2, hb, length),
            wide(block, width), wide(block, width),
            vmem(chunks, slots, 2 * hb, 5 * block), vmem(chunks, slots, 2 * hb, 5 * block),
            vmem(10 * hb, length),
            vmem(chunks, 2, 2, 2, *piece), vmem(chunks, 2, 2, *piece),
            vmem(chunks, 2, 2, *piece), vmem(chunks, 2, 2, *piece),
            vmem(2, EDGE, width), vmem(2, EDGE, width),
            dma(()), dma(()),
            dma((chunks, 3)), dma((chunks, 3)),
            dma((chunks, 2, 2)), dma((chunks, 2, 2)), dma((chunks,)),
            dma((2, 2)), dma((2, 2)),
            dma((chunks, slots)), dma((chunks, slots)), dma((chunks,)),
            dma((chunks, slots)), dma((chunks, slots)), dma((chunks,)),
            dma((chunks,)), dma((chunks,)),
            dma((chunks, 3)), dma((chunks, 3)), dma((chunks,)),
            dma((2,)), dma((2,)), dma((2,)),
        ],
        compiler_params=pltpu.CompilerParams(
            collective_id=0, has_side_effects=True, vmem_limit_bytes=52 * 2**20
        ),
        name="averaged_step",
    )(phase_index, weight_count, spectral_state, table)


CHUNK_ROWS = 16


def solution(mesh):
    in_specs = (P(None, None, "space", "avg"), P("avg"), P("avg"))
    out_specs = P(None, None, "space", "avg")
    body = cube_step if mesh.shape["avg"] == 4 else per_device
    return jax.shard_map(
        body, mesh=mesh, in_specs=in_specs, out_specs=out_specs, check_vma=False
    )
```

```python
import functools

import jax
import jax.numpy as jnp
import ml_dtypes
import numpy as np
from jax import lax
from jax.experimental import pallas as pl
from jax.experimental.pallas import tpu as pltpu
from jax.sharding import PartitionSpec as P

coriolis = 1.0
wave_speed = 6.0
phase_step = 0.25
time_step = 2.0
weight_scale = 4.0


def wave_of(positions, length):
    shifted = (positions + length // 2) % length - length // 2
    return shifted.astype(jnp.float32) * (2.0 / length)


def circle(products, length):
    angles = (products % length) * (2.0 * np.pi / length)
    return np.cos(angles).astype(np.float32), np.sin(angles).astype(np.float32)


def slot_base(slot, slots, half):
    return np.where(slot < slots // 2, 2 * half * slot, 2 * half * (slots - 1 - slot) + half)


def packed_table(length, slots, chunks):
    half = length // (2 * slots)
    rows = slot_base(np.arange(slots), slots, half)[:, None] + np.arange(half)
    cosine, sine = circle(rows[:, :, None] * np.arange(length), length)
    packed = np.stack([cosine, -sine], axis=1)
    packed[0, 1, 0] = circle(length // 2 * np.arange(length), length)[0]
    packed = packed.reshape(slots, 2, chunks, half // chunks, length).transpose(2, 0, 1, 3, 4)
    return packed.reshape(length, length).astype(ml_dtypes.bfloat16)


def turned(first, second):
    (c, s), (d, t) = first, second
    return c * d - s * t, s * d + c * t


def angle_tables(length, width, owners):
    y = np.arange(length)
    return [
        jnp.asarray(np.stack(circle(step * np.arange(count)[:, None] * y, length)))
        for step, count in ((width, owners), (FINE, width // FINE), (1, FINE))
    ]


def wave_operator(fields, kx, ky):
    (er, ei), (nr, ni), (hr, hi) = fields
    cx, cy = wave_speed * kx, wave_speed * ky
    return (
        (coriolis * nr + cx * hi, coriolis * ni - cx * hr),
        (cy * hi - coriolis * er, -coriolis * ei - cy * hr),
        (cx * ei + cy * ni, -(cx * er + cy * nr)),
    )


def wave_factors(kx, ky, phase):
    square = coriolis * coriolis + wave_speed * wave_speed * (kx * kx + ky * ky)
    frequency = jnp.sqrt(square)
    angle = frequency * phase
    return jnp.sin(angle) / frequency, (1.0 - jnp.cos(angle)) / square


def wave_exponential(fields, kx, ky, factors):
    sine, cosine = factors
    single = wave_operator(fields, kx, ky)
    double = wave_operator(single, kx, ky)
    return tuple(
        tuple(w + sine * a + cosine * b for w, a, b in zip(ws, one, two))
        for ws, one, two in zip(fields, single, double)
    )


def planes(fields):
    return tuple((fields[i, 0], fields[i, 1]) for i in range(fields.shape[0]))


MESH = pl.DeviceIdType.MESH
EDGE = 16
FINE = 16


def column(info, t, index):
    return info[t, :, index : index + 1]


def positions():
    g, a = lax.axis_index("space"), lax.axis_index("avg")
    return g, a, a // 2, a % 2


def edge_partner(g, slots):
    aligned = 1 - (g % (slots // 2) + slots // 2 - 1) // (slots // 2)
    return ((slots - g) % slots + aligned * (slots // 2)) % slots


def greet(slots, chips, edges):
    g, a, q, core = positions()
    barrier = pltpu.get_barrier_semaphore()
    peers = [((g + d) % slots, a) for d in range(1, slots)]
    peers += [(g, 2 * q + 1 - core)]
    peers += [(g, 2 * ((q + m) % chips) + core) for m in range(1, chips)]
    if edges:
        across = edge_partner(g, slots)
        peers += [
            (across, 2 * ((q + m) % chips) + (core + c) % 2)
            for c in range(2) for m in range(chips) if c or m
        ]
    for space, avg in peers:
        pl.semaphore_signal(
            barrier, inc=1, device_id={"space": space, "avg": avg}, device_id_type=MESH
        )
    pl.semaphore_wait(barrier, len(peers))


def sending(slots):
    return sorted(range(1, slots), key=lambda d: (-min(d, slots - d), d))


def remote(src, dst, send, recv, space, avg):
    return pltpu.make_async_remote_copy(
        src_ref=src, dst_ref=dst, send_sem=send, recv_sem=recv,
        device_id={"space": space, "avg": avg}, device_id_type=MESH,
    )


DIMS_NT = (((1,), (1,)), ((), ()))


def step_kernel(
    dims, state, into_rows, back_rows, info, ky, own_kx, phase, blocks, steps, fines, packed_hbm, result,
    moved, top, gx, eg, rows_c, rows_s, half, arr, arr_t, grid, products, packed, ct, st, sine, cosine,
    end_sine, end_cosine, fh, ret, lhs, stage, rsin, acc, xs, rx, fin, own, other, edge,
    ex_s, ex_r, eg_s, eg_r, x_s, x_r, c_s, c_r, a_s, a_r, l_s,
    b_s, b_r, m_s, d_s, d_r, y_s, y_r, gv_s, gv_r, le_s, le_r, bring_s,
):
    slots, chips, chunks, hb, width, block = dims
    length, reach = slots * block, block // 2
    g, a, q, core = positions()
    low, high = g < slots // 2, g >= slots // 2
    partner = 2 * q + 1 - core
    across = edge_partner(g, slots)
    side = g // (slots // 2)
    bring = pltpu.make_async_copy(packed_hbm, packed, bring_s)

    for f in range(3):
        for i in range(2):
            plane = state[f, i].astype(jnp.bfloat16)
            top[f, i] = plane[:EDGE]
            picked = jnp.dot(into_rows[side], plane, preferred_element_type=jnp.float32)
            picked = picked.astype(jnp.bfloat16)
            for s in range(2):
                for t in range(chunks):
                    spot = s * reach + t * hb
                    moved[s, t, f, i] = picked[spot : spot + hb]
    greet(slots, chips, True)

    def build_factors(unused):
        for t in range(chunks):
            for s in range(2):
                def one(j, carry, t=t, s=s):
                    span = pl.ds(pl.multiple_of(j * 256, 256), 256)
                    factors = wave_factors(column(info, t, s), ky[:, span], phase[...])
                    sine[t, s, :, span], cosine[t, s, :, span] = factors
                    return carry
                lax.fori_loop(0, length // 256, one, 0)

    def own_factors():
        end_sine[...], end_cosine[...] = wave_factors(own_kx[...], ky[:, :width], time_step)

    def build_tables():
        for c in range(2):
            for m in range(chips):
                owner = 2 * ((q + m) % chips) + (core + c) % 2
                first = (blocks[0, pl.ds(owner, 1), :], blocks[1, pl.ds(owner, 1), :])

                def one(h, carry, j=c * chips + m, first=first):
                    begin = turned(first, (steps[0, pl.ds(h, 1), :], steps[1, pl.ds(h, 1), :]))
                    cos_rows, sin_rows = turned(begin, (fines[0], fines[1]))
                    at = pl.ds(pl.multiple_of(j * width + h * FINE, FINE), FINE)
                    ct[at, :] = cos_rows.astype(jnp.bfloat16)
                    st[at, :] = sin_rows.astype(jnp.bfloat16)
                    return carry
                lax.fori_loop(0, width // FINE, one, 0)

    exchange = [
        remote(moved.at[1, t], gx.at[t, 1, 0, 0], ex_s.at[t], ex_r.at[t], slots - 1 - g, a)
        for t in range(chunks)
    ]
    edges = [
        remote(top, eg.at[c, m], eg_s.at[c, m], eg_r.at[c, m],
               across, 2 * ((q + chips - m) % chips) + (core + c) % 2)
        for c in range(2) for m in range(chips)
    ]

    def mine(t, s):
        return gx.at[t, 1, 0, 0] if s else moved.at[0, t]

    def over_chips(t, s, m):
        return remote(mine(t, s), gx.at[t, s, 0, m], x_s.at[t, s, m], x_r.at[t, s, m],
                      g, 2 * ((q + chips - m) % chips) + core)

    def over_cores(t, s, m):
        source = gx.at[t, s, 0, m] if m else mine(t, s)
        return remote(source, gx.at[t, s, 1, m], c_s.at[t, s, m], c_r.at[t, s, m], g, partner)

    def to_grid(t, d):
        to = (g + d) % slots
        return remote(half.at[t, to], arr.at[t, g], a_s.at[t, d], a_r.at[t, d], to, a)

    exchange[0].start()

    @pl.when(high)
    def _():
        for copy in edges:
            copy.start()
        eg[...] = jnp.zeros_like(eg)

    for t in range(1, chunks):
        exchange[t].start()
    for t in range(chunks):
        for m in range(1, chips):
            over_chips(t, 0, m).start()
        over_cores(t, 0, 0).start()
    bring.start()
    build_factors(0)
    build_tables()
    for t in range(chunks):
        for m in range(1, chips):
            over_chips(t, 0, m).wait_recv()
            over_cores(t, 0, m).start()
    def spread(t):
        exchange[t].wait_recv()
        for m in range(1, chips):
            over_chips(t, 1, m).start()
        over_cores(t, 1, 0).start()

    spread(0)
    for t in range(chunks):
        for m in range(1, chips):
            over_chips(t, 1, m).wait_recv()
            over_cores(t, 1, m).start()
        if t + 1 < chunks:
            spread(t + 1)
        if t == 0:
            @pl.when(low)
            def _():
                for copy in edges:
                    copy.wait_recv()
        for s in range(2):
            for m in range(chips):
                over_cores(t, s, m).wait_recv()
        own_pair = column(info, t, 2) > 0.5
        sign = column(info, t, 3)
        for j in range(2 * chips):
            c, m = divmod(j, chips)
            span = slice(j * width, (j + 1) * width)
            turned_rows = []
            for s in range(2):
                source = moved.at[0, t] if s + j == 0 else gx.at[t, s, c, m]
                fields = [[source[f, i].astype(jnp.float32) for i in range(2)] for f in range(3)]
                if s == 1 and t == 0:
                    put = column(info, t, 4)[:EDGE] > 0.5
                    for f in range(3):
                        for i in range(2):
                            top = jnp.where(put, eg[c, m, f, i].astype(jnp.float32), fields[f][i][:EDGE])
                            fields[f][i] = (
                                jnp.concatenate([top, fields[f][i][EDGE:]], axis=0) if hb > EDGE else top
                            )
                turned_rows.append(wave_exponential(
                    fields, column(info, t, s), ky[:, span], (sine[t, s, :, span], cosine[t, s, :, span])
                ))
            for f in range(3):
                (re0, im0), (re1, im1) = turned_rows[0][f], turned_rows[1][f]
                for i, value in enumerate((
                    jnp.where(own_pair, re0, re0 + re1), jnp.where(own_pair, re1, sign * (im0 - im1))
                )):
                    rows_c[(i * 3 + f) * hb : (i * 3 + f + 1) * hb, span] = value.astype(jnp.bfloat16)
                for i, value in enumerate((
                    jnp.where(own_pair, -im0, -(im0 + im1)), jnp.where(own_pair, -im1, sign * (re0 - re1))
                )):
                    rows_s[(i * 3 + f) * hb : (i * 3 + f + 1) * hb, span] = value.astype(jnp.bfloat16)
        tile = min(length, max(block, 256))
        for y in range(0, length, tile):
            value = (
                jnp.dot(rows_c[...], ct[:, y : y + tile], preferred_element_type=jnp.float32)
                + jnp.dot(rows_s[...], st[:, y : y + tile], preferred_element_type=jnp.float32)
            ).astype(jnp.bfloat16)
            for b in range(tile // block):
                for i in range(2):
                    for f in range(3):
                        half[t, y // block + b, i * hb : (i + 1) * hb, f * block : (f + 1) * block] = (
                            value[(i * 3 + f) * hb : (i * 3 + f + 1) * hb, b * block : (b + 1) * block]
                        )
        for d in sending(slots):
            to_grid(t, d).start()
        pltpu.make_async_copy(half.at[t, g], arr.at[t, g], l_s.at[t]).start()
    def to_rows(t, d):
        to = (g + d) % slots
        return remote(fh.at[t, to], ret.at[t, g], b_s.at[t, d], b_r.at[t, d], to, a)

    def sum_cores(t):
        return remote(stage.at[t, 1], rsin.at[t], d_s.at[t], d_r.at[t], g, partner)

    def sum_chips(t, m):
        return remote(xs.at[t, m], rx.at[t, m], y_s.at[t, m], y_r.at[t, m],
                      g, 2 * ((q + m) % chips) + core)

    def give(t):
        return remote(fin.at[t], other.at[t], gv_s.at[t], gv_r.at[t], slots - 1 - g, a)

    last = remote(fin.at[0, :, :, :EDGE], edge, le_s, le_r, edge_partner(g, slots), a)

    bring.wait()
    for t in range(chunks):
        for d in range(1, slots):
            to_grid(t, d).wait_recv()
        pltpu.make_async_copy(half.at[t, g], arr.at[t, g], l_s.at[t]).wait()
        together = max(1, 128 // (2 * hb))
        for p in range(0, slots, together):
            value = arr[t, p : p + together].astype(jnp.float32)
            value = value.reshape(together * 2 * hb, 3 * block)
            spot = p * 2 * hb
            arr_t[:, spot : spot + together * 2 * hb] = value.T.astype(jnp.bfloat16)
        depth = length // chunks
        for x in range(0, length, 256):
            value = jnp.dot(
                arr_t[...], packed[t * depth : (t + 1) * depth, x : x + 256],
                preferred_element_type=jnp.float32,
            )
            if t:
                value = value + grid[:, x : x + 256]
            if t < chunks - 1:
                grid[:, x : x + 256] = value
            else:
                value = value * (1.0 / length)
                east, north, height = (value[i * block : (i + 1) * block] for i in range(3))
                for k, pair in enumerate((
                    east * east, east * north, north * north, east * height, north * height
                )):
                    products[k * block : (k + 1) * block, x : x + 256] = pair.astype(jnp.bfloat16)
    for t in range(chunks):
        for k in range(0, depth, 256):
            value = lax.dot_general(
                packed[t * depth + k : t * depth + k + 256, :], products[...], DIMS_NT,
                preferred_element_type=jnp.float32,
            ).astype(jnp.bfloat16)
            for n in range(256 // (2 * hb)):
                fh[t, k // (2 * hb) + n] = value[n * 2 * hb : (n + 1) * 2 * hb]
        for d in sending(slots):
            to_rows(t, d).start()
        pltpu.make_async_copy(fh.at[t, g], ret.at[t, g], m_s.at[t]).start()
    own_factors()

    @pl.when(low)
    def _():
        edge[...] = jnp.zeros_like(edge)

    def finish(t):
        for m in range(1, chips):
            sum_chips(t, m).wait_recv()
            acc[...] += rx[t, m].astype(jnp.float32)
        fin[t] = acc[1].astype(jnp.bfloat16)
        give(t).start()
        if t == 0:
            @pl.when(low)
            def _():
                last.start()
        own[t] = acc[0].astype(jnp.bfloat16)

    for t in range(chunks):
        for d in range(1, slots):
            to_rows(t, d).wait_recv()
        pltpu.make_async_copy(fh.at[t, g], ret.at[t, g], m_s.at[t]).wait()
        for p in range(slots):
            for k in range(5):
                lhs[k * 2 * hb : (k + 1) * 2 * hb, p * block : (p + 1) * block] = (
                    ret[t, p, :, k * block : (k + 1) * block]
                )
        own_pair = column(info, t, 2) > 0.5
        sign, scale = column(info, t, 3), column(info, t, 5)
        for j in range(2 * chips):
            c, m = divmod(j, chips)
            span = slice(j * width, (j + 1) * width)
            by_c = lax.dot_general(lhs[...], ct[span, :], DIMS_NT, preferred_element_type=jnp.float32)
            by_s = lax.dot_general(lhs[...], st[span, :], DIMS_NT, preferred_element_type=jnp.float32)

            def part(values, k, i):
                return values[(2 * k + i) * hb : (2 * k + i + 1) * hb]

            for s in range(2):
                turn = scale * sign if s == 0 else -scale * sign
                real, imag = [], []
                for k in range(5):
                    rc, ic = part(by_c, k, 0), part(by_c, k, 1)
                    rs, iz = part(by_s, k, 0), part(by_s, k, 1)
                    real.append(jnp.where(own_pair, scale * (ic if s else rc), scale * rc + turn * iz))
                    imag.append(jnp.where(own_pair, -scale * (iz if s else rs), turn * ic - scale * rs))
                kx, kyj = column(info, t, s), ky[:, span]
                tendency = [
                    (kx * imag[u] + kyj * imag[v], -(kx * real[u] + kyj * real[v]))
                    for u, v in ((0, 1), (1, 2), (3, 4))
                ]
                back = wave_exponential(
                    tendency, kx, kyj, (-sine[t, s, :, span], cosine[t, s, :, span])
                )
                for f in range(3):
                    for i in range(2):
                        stage[t, c, m, s, f, i] = back[f][i].astype(jnp.bfloat16)
        sum_cores(t).start()
        if t:
            finish(t - 1)
        sum_cores(t).wait_recv()
        for m in range(1, chips):
            xs[t, m] = (
                stage[t, 0, m].astype(jnp.float32) + rsin[t, m].astype(jnp.float32)
            ).astype(jnp.bfloat16)
            sum_chips(t, m).start()
        acc[...] = stage[t, 0, 0].astype(jnp.float32) + rsin[t, 0].astype(jnp.float32)
    finish(chunks - 1)
    for t in range(chunks):
        give(t).wait_recv()

    @pl.when(high)
    def _():
        last.wait_recv()

    for t in range(chunks):
        exchange[t].wait_send()
        for s in range(2):
            for m in range(1, chips):
                over_chips(t, s, m).wait_send()
            for m in range(chips):
                over_cores(t, s, m).wait_send()
        for d in range(1, slots):
            to_grid(t, d).wait_send()

    @pl.when(high)
    def _():
        for copy in edges:
            copy.wait_send()


    for t in range(chunks):
        for d in range(1, slots):
            to_rows(t, d).wait_send()
        sum_cores(t).wait_send()
        for m in range(1, chips):
            sum_chips(t, m).wait_send()
        give(t).wait_send()

    @pl.when(low)
    def _():
        last.wait_send()


    for f in range(3):
        for i in range(2):
            rows = jnp.concatenate(
                [own[t, f, i] for t in range(chunks)] + [other[t, f, i] for t in range(chunks)]
                + [edge[f, i]], axis=0,
            )
            averaged = jnp.dot(back_rows[side], rows, preferred_element_type=jnp.float32)
            result[f, i] = state[f, i] + time_step * averaged
    fields = [[result[f, i] for i in range(2)] for f in range(3)]
    advanced = wave_exponential(fields, own_kx[...], ky[:, :width], (end_sine[...], end_cosine[...]))
    for f in range(3):
        for i in range(2):
            result[f, i] = advanced[f][i]


VMEM = pl.BlockSpec(memory_space=pltpu.VMEM)


def per_device(spectral_state, phase_index, weight_count):
    slots, owners = lax.axis_size("space"), lax.axis_size("avg")
    block, width = spectral_state.shape[2:]
    length, half = block * slots, block // 2
    chips = owners // 2
    chunks = max(1, half // CHUNK_ROWS)
    hb = half // chunks
    dims = (slots, chips, chunks, hb, width, block)
    g, a = lax.axis_index("space"), lax.axis_index("avg")
    q, core = a // 2, a % 2
    low = g < slots // 2
    phase = phase_index[0].astype(jnp.float32) * phase_step
    weight = weight_count[0].astype(jnp.float32) / (weight_scale * owners)

    m, c = jnp.arange(chips, dtype=jnp.int32), jnp.arange(2, dtype=jnp.int32)[:, None]
    order = (2 * ((q + m) % chips) + (core + c) % 2).reshape(-1)
    columns = (order[:, None] * width + jnp.arange(width, dtype=jnp.int32)).reshape(1, -1)
    ky = wave_of(columns, length)
    packed = jnp.asarray(packed_table(length, slots, chunks))

    base = jnp.where(low, 2 * half * g, 2 * half * (slots - 1 - g) + half)
    direct = base + jnp.arange(half, dtype=jnp.int32)
    mirror = jnp.where(direct == 0, length // 2, length - direct)
    first = wave_of(jnp.where(low, direct, mirror), length)
    second = wave_of(jnp.where(low, mirror, direct), length)
    ones = jnp.ones((half,), jnp.float32)
    start = (jnp.arange(half) == 0) & low
    info = jnp.stack([
        first, second, (direct == 0).astype(jnp.float32), jnp.where(low, ones, -ones),
        start.astype(jnp.float32), ones * (weight / length), ones, ones,
    ], axis=1).reshape(chunks, hb, 8)
    own_kx = wave_of(g * block + jnp.arange(block, dtype=jnp.int32)[:, None], length)

    r = np.arange(half)
    into = np.zeros((2, 2, half, block), np.float32)
    into[0, 0, r, r] = 1
    into[0, 1, r, half + r] = 1
    into[1, 0, r, half - r] = 1
    into[1, 1, r[1:], block - r[1:]] = 1
    into = jnp.asarray(into.reshape(2, block, block).astype(ml_dtypes.bfloat16))
    back = np.zeros((2, block, 2 * half + EDGE), np.float32)
    back[0, r, r] = 1
    back[0, half + r, half + r] = 1
    back[1, half - r, r] = 1
    back[1, block - r[1:], half + r[1:]] = 1
    back[1, 0, 2 * half] = 1
    back = jnp.asarray(back.astype(ml_dtypes.bfloat16))

    piece = (3, 2, hb, width)
    dma = pltpu.SemaphoreType.DMA
    vmem = lambda *shape: pltpu.VMEM(shape, jnp.bfloat16)
    wide = lambda *shape: pltpu.VMEM(shape, jnp.float32)
    return pl.pallas_call(
        functools.partial(step_kernel, dims),
        out_shape=jax.ShapeDtypeStruct(spectral_state.shape, jnp.float32),
        in_specs=[VMEM] * 10 + [pl.BlockSpec(memory_space=pl.ANY)],
        out_specs=VMEM,
        scratch_shapes=[
            vmem(2, chunks, *piece), vmem(3, 2, EDGE, width),
            vmem(chunks, 2, 2, chips, *piece), vmem(2, chips, 3, 2, EDGE, width),
            vmem(6 * hb, length), vmem(6 * hb, length),
            vmem(chunks, slots, 2 * hb, 3 * block), vmem(chunks, slots, 2 * hb, 3 * block),
            vmem(3 * block, length // chunks), wide(3 * block, length), vmem(5 * block, length),
            vmem(length, length), vmem(length, length), vmem(length, length),
            wide(chunks, 2, hb, length), wide(chunks, 2, hb, length),
            wide(block, width), wide(block, width),
            vmem(chunks, slots, 2 * hb, 5 * block), vmem(chunks, slots, 2 * hb, 5 * block),
            vmem(10 * hb, length),
            vmem(chunks, 2, chips, 2, *piece), vmem(chunks, chips, 2, *piece),
            wide(2, *piece), vmem(chunks, chips, 2, *piece), vmem(chunks, chips, 2, *piece),
            vmem(chunks, *piece), vmem(chunks, *piece), vmem(chunks, *piece),
            vmem(3, 2, EDGE, width),
            dma((chunks,)), dma((chunks,)),
            dma((2, chips)), dma((2, chips)),
            dma((chunks, 2, chips)), dma((chunks, 2, chips)),
            dma((chunks, 2, chips)), dma((chunks, 2, chips)),
            dma((chunks, slots)), dma((chunks, slots)), dma((chunks,)),
            dma((chunks, slots)), dma((chunks, slots)), dma((chunks,)),
            dma((chunks,)), dma((chunks,)),
            dma((chunks, chips)), dma((chunks, chips)),
            dma((chunks,)), dma((chunks,)),
            dma(()), dma(()), dma(()),
        ],
        compiler_params=pltpu.CompilerParams(
            collective_id=0, has_side_effects=True, vmem_limit_bytes=56 * 2**20
        ),
        name="averaged_step",
    )(spectral_state, into, back, info, ky, own_kx, phase.reshape(1, 1),
      *angle_tables(length, width, owners), packed)


def signal_all(barrier, peers):
    for space, avg in peers:
        pl.semaphore_signal(
            barrier, inc=1, device_id={"space": space, "avg": avg}, device_id_type=MESH
        )


def only_row(n, value, rows):
    spot = lax.broadcasted_iota(jnp.int32, (rows, value.shape[-1]), 0)
    return jnp.where(spot == n, jnp.broadcast_to(value, (rows, value.shape[-1])), 0.0)


def cube_kernel(
    dims, phase_ref, weight_ref, state_hbm, table_hbm, result,
    state, order_rows, info, ky, own_kx, parts, ph_mine, ph_got, moved, top, gx, eg, rows_c, rows_s, half, arr, arr_t, grid, products, packed,
    ct, st, sine, cosine, end_sine, end_cosine, fh, ret, lhs, stage, rsin, xs, rb, lt, le,
    ph_s, ph_r, x_s, x_r, c_s, c_r, g_s, eg_s, eg_r, a_s, a_r, l_s,
    b_s, b_r, m_s, d_s, d_r, y_s, y_r, k_s, le_s, le_r, load_s,
):
    slots, chunks, hb, width, block = dims
    length, reach = slots * block, block // 2
    g, a, q, core = positions()
    side = g // (slots // 2)
    pair_block = g + side * (slots - 1 - 2 * g)
    me = 2 * pair_block + q
    mirror = slots - 1 - g
    partner = 2 * q + 1 - core
    low, high = side == 0, side == 1

    def place(slot):
        b = slot // 2
        return b + side * (slots - 1 - 2 * b), 2 * (slot % 2) + core

    def chip(m):
        return (q + m) % 2

    barrier = pltpu.get_barrier_semaphore()
    near = [place((me + d) % slots) for d in range(1, slots)] + [(g, partner)]
    near += [(mirror, 2 * chip(m) + core) for m in range(2)]
    across = edge_partner(g, slots)
    below = [(across, c) for c in range(2)] + [(slots - 1 - across, c) for c in range(2)]
    source = edge_partner(pair_block, slots)
    above = [(source, c) for c in range(4)]
    signal_all(barrier, near)

    @pl.when(high)
    def _():
        signal_all(barrier, below)

    @pl.when(q == 0)
    def _():
        signal_all(barrier, above)
    loads = [
        pltpu.make_async_copy(source_ref, target, load_s.at[n])
        for n, (source_ref, target) in enumerate((
            (state_hbm, state), (table_hbm, parts)
        ))
    ]
    for copy in loads:
        copy.start()

    def wave(spot):
        return jnp.where(spot >= length // 2, spot - length, spot).astype(jnp.float32) * (2.0 / length)

    lane = lax.broadcasted_iota(jnp.int32, (hb, 128), 1)
    for t in range(chunks):
        spot = lax.broadcasted_iota(jnp.int32, (hb, 128), 0) + t * hb
        direct = spot + (block * pair_block + reach * q)
        mirrored = jnp.where(direct == 0, length // 2, length - direct)
        begins = jnp.where(spot == 0, 1.0, 0.0)
        info[t] = jnp.where(lane == 0, wave(direct), jnp.where(lane == 1, wave(mirrored), jnp.where(
            lane == 2, jnp.where(direct == 0, 1.0, 0.0), jnp.where(
                lane == 3, begins * (1 - q).astype(jnp.float32), begins * side.astype(jnp.float32)
            )
        )))
    own_kx[...] = wave(lax.broadcasted_iota(jnp.int32, (block, 128), 0) + g * block)
    for j in range(4):
        c, m = divmod(j, 2)
        owner = 2 * ((q + m) % 2) + (core + c) % 2
        spot = lax.broadcasted_iota(jnp.int32, (1, width), 1) + owner * width
        ky[:, j * width : (j + 1) * width] = wave(spot)
    down = lax.broadcasted_iota(jnp.int32, (block, block), 0)
    along = lax.broadcasted_iota(jnp.int32, (block, block), 1)
    turned_down = jnp.where(down == 0, 0, block - down)
    order_rows[...] = jnp.where(
        along == down + side * (turned_down - down), 1.0, 0.0
    ).astype(jnp.bfloat16)
    lane = lax.broadcasted_iota(jnp.int32, ph_mine.shape, 1)
    ph_mine[...] = jnp.where(
        lane == 0, phase_ref[0].astype(jnp.float32) * phase_step,
        weight_ref[0].astype(jnp.float32) / (weight_scale * 4),
    )
    loads[0].wait()

    top_tile = jnp.zeros((EDGE, width), jnp.float32)
    for f in range(3):
        for i in range(2):
            plane = state[f, i].astype(jnp.bfloat16)
            top_tile = top_tile + only_row(2 * f + i, state[f, i, 0:1, :], EDGE)
            picked = jnp.dot(order_rows[...], plane, preferred_element_type=jnp.float32)
            picked = picked.astype(jnp.bfloat16)
            for h in range(2):
                for t in range(chunks):
                    spot = h * reach + t * hb
                    moved[h, t, f, i] = picked[spot : spot + hb]
    top[...] = top_tile.astype(jnp.bfloat16)
    pl.semaphore_wait(barrier, len(near) + len(below) * side + len(above) * (1 - q))

    def build_factors(t):
        turn = chosen_phase()[:, 0:1]
        if True:
            for s in range(2):
                def one(j, carry, t=t, s=s):
                    span = pl.ds(pl.multiple_of(j * 256, 256), 256)
                    factors = wave_factors(column(info, t, s), ky[:, span], turn)
                    sine[t, s, :, span], cosine[t, s, :, span] = factors
                    return carry
                lax.fori_loop(0, length // 256, one, 0)

    def chosen_phase():
        keep = 1.0 - jnp.abs(q - side).astype(jnp.float32)
        return ph_got[0:1] + keep * (ph_mine[0:1] - ph_got[0:1])

    steps, owners = width // FINE, 4

    def begin_rows(owner, h):
        return turned(
            (parts[pl.ds(2 * (FINE + steps) + owner, 1)], parts[pl.ds(2 * (FINE + steps) + owners + owner, 1)]),
            (parts[pl.ds(2 * FINE + h, 1)], parts[pl.ds(2 * FINE + steps + h, 1)]),
        )

    def fine_rows(begin):
        return turned(begin, (parts[0:FINE], parts[FINE : 2 * FINE]))

    def build_packed():
        def one(n, carry):
            begin = begin_rows(n // steps, n % steps)
            cos_rows, sin_rows = fine_rows(begin)
            slot, t = n // chunks, n % chunks
            at = pl.multiple_of((t * slots + slot) * 2 * hb, 2 * hb)
            packed[pl.ds(at, hb), :] = cos_rows.astype(jnp.bfloat16)
            packed[pl.ds(at + hb, hb), :] = (-sin_rows).astype(jnp.bfloat16)
            return carry
        lax.fori_loop(0, length // (2 * FINE), one, 0)
        down = lax.broadcasted_iota(jnp.int32, (hb, length), 0)
        along = lax.broadcasted_iota(jnp.int32, (hb, length), 1)
        rest = packed[hb : 2 * hb, :].astype(jnp.float32)
        packed[hb : 2 * hb, :] = jnp.where(
            down == 0, 1.0 - 2.0 * (along % 2).astype(jnp.float32), rest
        ).astype(jnp.bfloat16)

    def build_tables():
        for c in range(2):
            for m in range(2):
                owner = 2 * chip(m) + (core + c) % 2

                def one(h, carry, j=c * 2 + m, owner=owner):
                    cos_rows, sin_rows = fine_rows(begin_rows(owner, h))
                    at = pl.ds(pl.multiple_of(j * width + h * FINE, FINE), FINE)
                    ct[at, :] = cos_rows.astype(jnp.bfloat16)
                    st[at, :] = sin_rows.astype(jnp.bfloat16)
                    return carry
                lax.fori_loop(0, width // FINE, one, 0)

    swap_phase = remote(ph_mine, ph_got, ph_s, ph_r, g, 2 * chip(1) + core)

    def bring_own(t):
        return remote(moved.at[chip(1), t], gx.at[t, side, 0, 1], x_s.at[t, 0], x_r.at[t, 0],
                      g, 2 * chip(1) + core)

    def bring_mirror(t, m):
        return remote(moved.at[chip(m), t], gx.at[t, side, 0, m], x_s.at[t, 1 + m], x_r.at[t, 1 + m],
                      mirror, 2 * chip(m) + core)

    def keep_own(t):
        return pltpu.make_async_copy(moved.at[q, t], gx.at[t, side, 0, 0], g_s.at[t])

    def over_cores(t, kind, m):
        role = (1 - side) if kind else side
        piece = gx.at[t, role, 0, m] if kind + m else moved.at[q, t]
        return remote(piece, gx.at[t, role, 1, m], c_s.at[t, kind, m], c_r.at[t, kind, m], g, partner)

    edges = [
        remote(top, eg.at[c, q], eg_s.at[k, c], eg_r.at[c, q], space, (core + c) % 2)
        for k, space in enumerate((across, slots - 1 - across)) for c in range(2)
    ]

    def to_grid(t, d):
        to = (me + d) % slots
        space, avg = place(to)
        return remote(half.at[t, to], arr.at[t, me], a_s.at[t, d], a_r.at[t, d], space, avg)

    def to_rows(t, d):
        to = (me + d) % slots
        space, avg = place(to)
        return remote(fh.at[t, to], ret.at[t, me], b_s.at[t, d], b_r.at[t, d], space, avg)

    def sum_cores(t):
        return remote(stage.at[t, 1], rsin.at[t], d_s.at[t], d_r.at[t], g, partner)

    def give_own(t):
        return remote(xs.at[t, 1, side], rb.at[t, 0, q], y_s.at[t, 0], y_r.at[t, 0],
                      g, 2 * chip(1) + core)

    def give_mirror(t, m):
        return remote(xs.at[t, m, 1 - side], rb.at[t, 1, q], y_s.at[t, 1 + m], y_r.at[t, 1 + m],
                      mirror, 2 * chip(m) + core)

    def give_self(t):
        return pltpu.make_async_copy(xs.at[t, 0, side], rb.at[t, 0, q], k_s.at[t])

    last = [
        remote(lt.at[m], le.at[side], le_s.at[m], le_r.at[side], source, 2 * chip(m) + core)
        for m in range(2)
    ]

    swap_phase.start()

    @pl.when(high)
    def _():
        for copy in edges:
            copy.start()
    def launch(t):
        for m in range(2):
            bring_mirror(t, m).start()
        bring_own(t).start()
        over_cores(t, 0, 0).start()
        keep_own(t).start()

    launch(0)
    pass
    @pl.when(q != 0)
    def _():
        eg[...] = jnp.zeros_like(eg)

    @pl.when(low)
    def _():
        le[...] = jnp.zeros_like(le)
    swap_phase.wait_recv()
    scale = chosen_phase()[:, 1:2] * (1.0 / length)

    def meet_edges():
        @pl.when(q == 0)
        def _():
            for c in range(2):
                for m in range(2):
                    remote(top, eg.at[c, m], eg_s.at[0, c], eg_r.at[c, m], g, partner).wait_recv()

    def rotate(t):
        bring_own(t).wait_recv()
        over_cores(t, 0, 1).start()
        for m in range(2):
            bring_mirror(t, m).wait_recv()
            over_cores(t, 1, m).start()
        keep_own(t).wait()
        for kind in range(2):
            for m in range(2):
                over_cores(t, kind, m).wait_recv()
        own_pair = column(info, t, 2) > 0.5
        for j in range(4):
            c, m = divmod(j, 2)
            span = slice(j * width, (j + 1) * width)
            turned_rows = []
            for s in range(2):
                piece = gx.at[t, s, c, m]
                fields = [[piece[f, i].astype(jnp.float32) for i in range(2)] for f in range(3)]
                if s == 1 and t == 0:
                    put = column(info, t, 3) > 0.5
                    tile = eg[c, m].astype(jnp.float32)
                    for f in range(3):
                        for i in range(2):
                            n = 2 * f + i
                            row = jnp.broadcast_to(tile[n : n + 1], (hb, width))
                            fields[f][i] = jnp.where(put, row, fields[f][i])
                turned_rows.append(wave_exponential(
                    fields, column(info, t, s), ky[:, span], (sine[t, s, :, span], cosine[t, s, :, span])
                ))
            for f in range(3):
                (re0, im0), (re1, im1) = turned_rows[0][f], turned_rows[1][f]
                for i, value in enumerate((
                    jnp.where(own_pair, re0, re0 + re1), jnp.where(own_pair, re1, im0 - im1)
                )):
                    rows_c[(i * 3 + f) * hb : (i * 3 + f + 1) * hb, span] = value.astype(jnp.bfloat16)
                for i, value in enumerate((
                    jnp.where(own_pair, -im0, -(im0 + im1)), jnp.where(own_pair, -im1, re0 - re1)
                )):
                    rows_s[(i * 3 + f) * hb : (i * 3 + f + 1) * hb, span] = value.astype(jnp.bfloat16)
        tile = min(length, max(block, 256))
        for y in range(0, length, tile):
            value = (
                jnp.dot(rows_c[...], ct[:, y : y + tile], preferred_element_type=jnp.float32)
                + jnp.dot(rows_s[...], st[:, y : y + tile], preferred_element_type=jnp.float32)
            ).astype(jnp.bfloat16)
            for b in range(tile // block):
                for i in range(2):
                    for f in range(3):
                        half[t, y // block + b, i * hb : (i + 1) * hb, f * block : (f + 1) * block] = (
                            value[(i * 3 + f) * hb : (i * 3 + f + 1) * hb, b * block : (b + 1) * block]
                        )
        for d in sending(slots):
            to_grid(t, d).start()
        pltpu.make_async_copy(half.at[t, me], arr.at[t, me], l_s.at[t]).start()

    depth = length // chunks

    def send_rows(t):
        for d in sending(slots):
            to_rows(t, d).start()
        pltpu.make_async_copy(fh.at[t, me], ret.at[t, me], m_s.at[t]).start()

    def on_grid(t):
        for d in range(1, slots):
            to_grid(t, d).wait_recv()
        pltpu.make_async_copy(half.at[t, me], arr.at[t, me], l_s.at[t]).wait()
        together = max(1, 128 // (2 * hb))
        for p in range(0, slots, together):
            value = arr[t, p : p + together].astype(jnp.float32)
            value = value.reshape(together * 2 * hb, 3 * block)
            spot = p * 2 * hb
            arr_t[:, spot : spot + together * 2 * hb] = value.T.astype(jnp.bfloat16)
        for x in range(0, length, 256):
            value = jnp.dot(
                arr_t[...], packed[t * depth : (t + 1) * depth, x : x + 256],
                preferred_element_type=jnp.float32,
            )
            if t:
                value = value + grid[:, x : x + 256]
            if t < chunks - 1:
                grid[:, x : x + 256] = value
            else:
                value = value * (1.0 / length)
                east, north, height = (value[i * block : (i + 1) * block] for i in range(3))
                for k, pair in enumerate((
                    east * east, east * north, north * north, east * height, north * height
                )):
                    products[k * block : (k + 1) * block, x : x + 256] = pair.astype(jnp.bfloat16)

    loads[1].wait()
    build_tables()
    build_factors(0)
    launch(1)
    build_factors(1)
    meet_edges()
    rotate(0)
    launch(2)
    build_packed()
    build_factors(2)
    rotate(1)
    launch(3)
    on_grid(0)
    build_factors(3)
    rotate(2)
    on_grid(1)
    rotate(3)
    on_grid(2)
    end_sine[...], end_cosine[...] = wave_factors(own_kx[:, 0:1], ky[:, :width], time_step)
    on_grid(chunks - 1)

    for t in range(chunks):
        for k in range(0, depth, 256):
            value = lax.dot_general(
                packed[t * depth + k : t * depth + k + 256, :], products[...], DIMS_NT,
                preferred_element_type=jnp.float32,
            ).astype(jnp.bfloat16)
            for n in range(256 // (2 * hb)):
                fh[t, k // (2 * hb) + n] = value[n * 2 * hb : (n + 1) * 2 * hb]
        if t < 2:
            send_rows(t)

    def pass_on(t):
        sum_cores(t).wait_recv()
        for m in range(2):
            for s in range(2):
                value = stage[t, 0, m, s].astype(jnp.float32) + rsin[t, m, s].astype(jnp.float32)
                xs[t, m, s] = value.astype(jnp.bfloat16)
                if t == 0 and s == 1:
                    tile = jnp.zeros((EDGE, width), jnp.float32)
                    for f in range(3):
                        for i in range(2):
                            tile = tile + only_row(2 * f + i, value[f, i, 0:1], EDGE)
                    lt[m] = tile.astype(jnp.bfloat16)
        for m in range(2):
            give_mirror(t, m).start()
        give_own(t).start()
        give_self(t).start()
        if t == 0:
            @pl.when(q == 0)
            def _():
                for copy in last:
                    copy.start()

    for t in range(chunks):
        for d in range(1, slots):
            to_rows(t, d).wait_recv()
        pltpu.make_async_copy(fh.at[t, me], ret.at[t, me], m_s.at[t]).wait()
        if t + 2 < chunks:
            send_rows(t + 2)
        for p in range(slots):
            for k in range(5):
                lhs[k * 2 * hb : (k + 1) * 2 * hb, p * block : (p + 1) * block] = (
                    ret[t, p, :, k * block : (k + 1) * block]
                )
        own_pair = column(info, t, 2) > 0.5
        for j in (2, 3, 0, 1):
            c, m = divmod(j, 2)
            if j == 0:
                sum_cores(t).start()
            span = slice(j * width, (j + 1) * width)
            by_c = lax.dot_general(lhs[...], ct[span, :], DIMS_NT, preferred_element_type=jnp.float32)
            by_s = lax.dot_general(lhs[...], st[span, :], DIMS_NT, preferred_element_type=jnp.float32)

            def part(values, k, i):
                return values[(2 * k + i) * hb : (2 * k + i + 1) * hb] * scale

            for s in range(2):
                real, imag = [], []
                for k in range(5):
                    rc, ic = part(by_c, k, 0), part(by_c, k, 1)
                    rs, iz = part(by_s, k, 0), part(by_s, k, 1)
                    real.append(jnp.where(own_pair, (ic if s else rc), (rc - iz if s else rc + iz)))
                    imag.append(jnp.where(own_pair, -(iz if s else rs), (-ic if s else ic) - rs))
                kx, kyj = column(info, t, s), ky[:, span]
                tendency = [
                    (kx * imag[u] + kyj * imag[v], -(kx * real[u] + kyj * real[v]))
                    for u, v in ((0, 1), (1, 2), (3, 4))
                ]
                back = wave_exponential(
                    tendency, kx, kyj, (-sine[t, s, :, span], cosine[t, s, :, span])
                )
                for f in range(3):
                    for i in range(2):
                        stage[t, c, m, s, f, i] = back[f][i].astype(jnp.bfloat16)
        pass_on(t)

    for t in range(chunks):
        bring_own(t).wait_send()
        for m in range(2):
            bring_mirror(t, m).wait_send()
        for kind in range(2):
            for m in range(2):
                over_cores(t, kind, m).wait_send()
        for d in range(1, slots):
            to_grid(t, d).wait_send()
            to_rows(t, d).wait_send()
        sum_cores(t).wait_send()
    swap_phase.wait_send()

    @pl.when(high)
    def _():
        for copy in edges:
            copy.wait_send()
        for k in range(2):
            remote(lt.at[0], le.at[k], le_s.at[0], le_r.at[k], g, partner).wait_recv()

    for t in range(chunks):
        give_own(t).wait_recv()
        for m in range(2):
            give_mirror(t, m).wait_recv()
        give_self(t).wait()

    edge = le[0].astype(jnp.float32) + le[1].astype(jnp.float32)
    for f in range(3):
        for i in range(2):
            pieces = [
                rb[t, 0, h, f, i].astype(jnp.float32) + rb[t, 1, h, f, i].astype(jnp.float32)
                for h in range(2) for t in range(chunks)
            ]
            n = 2 * f + i
            pieces[0] = jnp.where(
                column(info, 0, 4) > 0.5, jnp.broadcast_to(edge[n : n + 1], (hb, width)), pieces[0]
            )
            rows = jnp.concatenate(pieces, axis=0).astype(jnp.bfloat16)
            averaged = jnp.dot(order_rows[...], rows, preferred_element_type=jnp.float32)
            result[f, i] = state[f, i] * (1.0 / time_step) + averaged
    fields = [[result[f, i] for i in range(2)] for f in range(3)]
    advanced = wave_exponential(fields, own_kx[:, 0:1], ky[:, :width], (end_sine[...], end_cosine[...]))
    for f in range(3):
        for i in range(2):
            result[f, i] = advanced[f][i]

    for t in range(chunks):
        give_own(t).wait_send()
        for m in range(2):
            give_mirror(t, m).wait_send()

    @pl.when(q == 0)
    def _():
        for copy in last:
            copy.wait_send()


def cube_step(spectral_state, phase_index, weight_count):
    slots, owners = lax.axis_size("space"), lax.axis_size("avg")
    block, width = spectral_state.shape[2:]
    length, half = block * slots, block // 2
    chunks = max(1, half // CHUNK_ROWS)
    hb = half // chunks
    dims = (slots, chunks, hb, width, block)
    spans = ((1, FINE), (FINE, width // FINE), (width, owners))
    table = np.concatenate([
        part for step, count in spans
        for part in circle(step * np.arange(count)[:, None] * np.arange(length), length)
    ])
    table = jnp.asarray(table)
    piece = (3, 2, hb, width)
    dma = pltpu.SemaphoreType.DMA
    vmem = lambda *shape: pltpu.VMEM(shape, jnp.bfloat16)
    wide = lambda *shape: pltpu.VMEM(shape, jnp.float32)
    return time_step * pl.pallas_call(
        functools.partial(cube_kernel, dims),
        out_shape=jax.ShapeDtypeStruct(spectral_state.shape, jnp.float32),
        in_specs=[pl.BlockSpec(memory_space=pltpu.SMEM)] * 2 + [pl.BlockSpec(memory_space=pltpu.HBM)] * 2,
        out_specs=VMEM,
        scratch_shapes=[
            wide(3, 2, block, width), vmem(block, block), wide(chunks, hb, 128), wide(1, length),
            wide(block, 128), wide(*table.shape),
            wide(8, 128), wide(8, 128),
            vmem(2, chunks, *piece), vmem(EDGE, width),
            vmem(chunks, 2, 2, 2, *piece), vmem(2, 2, EDGE, width),
            vmem(6 * hb, length), vmem(6 * hb, length),
            vmem(chunks, slots, 2 * hb, 3 * block), vmem(chunks, slots, 2 * hb, 3 * block),
            vmem(3 * block, length // chunks), wide(3 * block, length), vmem(5 * block, length),
            vmem(length, length), vmem(length, length), vmem(length, length),
            wide(chunks, 2, hb, length), wide(chunks, 2, hb, length),
            wide(block, width), wide(block, width),
            vmem(chunks, slots, 2 * hb, 5 * block), vmem(chunks, slots, 2 * hb, 5 * block),
            vmem(10 * hb, length),
            vmem(chunks, 2, 2, 2, *piece), vmem(chunks, 2, 2, *piece),
            vmem(chunks, 2, 2, *piece), vmem(chunks, 2, 2, *piece),
            vmem(2, EDGE, width), vmem(2, EDGE, width),
            dma(()), dma(()),
            dma((chunks, 3)), dma((chunks, 3)),
            dma((chunks, 2, 2)), dma((chunks, 2, 2)), dma((chunks,)),
            dma((2, 2)), dma((2, 2)),
            dma((chunks, slots)), dma((chunks, slots)), dma((chunks,)),
            dma((chunks, slots)), dma((chunks, slots)), dma((chunks,)),
            dma((chunks,)), dma((chunks,)),
            dma((chunks, 3)), dma((chunks, 3)), dma((chunks,)),
            dma((2,)), dma((2,)), dma((2,)),
        ],
        compiler_params=pltpu.CompilerParams(
            collective_id=0, has_side_effects=True, vmem_limit_bytes=105 * 2**19
        ),
        name="averaged_step",
    )(phase_index, weight_count, spectral_state, table)


CHUNK_ROWS = 16


def solution(mesh):
    in_specs = (P(None, None, "space", "avg"), P("avg"), P("avg"))
    out_specs = P(None, None, "space", "avg")
    body = cube_step if mesh.shape["avg"] == 4 else per_device
    return jax.shard_map(
        body, mesh=mesh, in_specs=in_specs, out_specs=out_specs, check_vma=False
    )
```

```python
import functools

import jax
import jax.numpy as jnp
import ml_dtypes
import numpy as np
from jax import lax
from jax.experimental import pallas as pl
from jax.experimental.pallas import tpu as pltpu
from jax.sharding import PartitionSpec as P

coriolis = 1.0
wave_speed = 6.0
phase_step = 0.25
time_step = 2.0
weight_scale = 4.0


def wave_of(positions, length):
    shifted = (positions + length // 2) % length - length // 2
    return shifted.astype(jnp.float32) * (2.0 / length)


def circle(products, length):
    angles = (products % length) * (2.0 * np.pi / length)
    return np.cos(angles).astype(np.float32), np.sin(angles).astype(np.float32)


def slot_base(slot, slots, half):
    return np.where(slot < slots // 2, 2 * half * slot, 2 * half * (slots - 1 - slot) + half)


def packed_table(length, slots, chunks):
    half = length // (2 * slots)
    rows = slot_base(np.arange(slots), slots, half)[:, None] + np.arange(half)
    cosine, sine = circle(rows[:, :, None] * np.arange(length), length)
    packed = np.stack([cosine, -sine], axis=1)
    packed[0, 1, 0] = circle(length // 2 * np.arange(length), length)[0]
    packed = packed.reshape(slots, 2, chunks, half // chunks, length).transpose(2, 0, 1, 3, 4)
    return packed.reshape(length, length).astype(ml_dtypes.bfloat16)


def turned(first, second):
    (c, s), (d, t) = first, second
    return c * d - s * t, s * d + c * t


def angle_tables(length, width, owners):
    y = np.arange(length)
    return [
        jnp.asarray(np.stack(circle(step * np.arange(count)[:, None] * y, length)))
        for step, count in ((width, owners), (FINE, width // FINE), (1, FINE))
    ]


def wave_operator(fields, kx, ky):
    (er, ei), (nr, ni), (hr, hi) = fields
    cx, cy = wave_speed * kx, wave_speed * ky
    return (
        (coriolis * nr + cx * hi, coriolis * ni - cx * hr),
        (cy * hi - coriolis * er, -coriolis * ei - cy * hr),
        (cx * ei + cy * ni, -(cx * er + cy * nr)),
    )


def wave_factors(kx, ky, phase):
    square = coriolis * coriolis + wave_speed * wave_speed * (kx * kx + ky * ky)
    frequency = jnp.sqrt(square)
    angle = frequency * phase
    return jnp.sin(angle) / frequency, (1.0 - jnp.cos(angle)) / square


def wave_exponential(fields, kx, ky, factors):
    sine, cosine = factors
    single = wave_operator(fields, kx, ky)
    double = wave_operator(single, kx, ky)
    return tuple(
        tuple(w + sine * a + cosine * b for w, a, b in zip(ws, one, two))
        for ws, one, two in zip(fields, single, double)
    )


def planes(fields):
    return tuple((fields[i, 0], fields[i, 1]) for i in range(fields.shape[0]))


MESH = pl.DeviceIdType.MESH
EDGE = 16
FINE = 16


def column(info, t, index):
    return info[t, :, index : index + 1]


def positions():
    g, a = lax.axis_index("space"), lax.axis_index("avg")
    return g, a, a // 2, a % 2


def edge_partner(g, slots):
    aligned = 1 - (g % (slots // 2) + slots // 2 - 1) // (slots // 2)
    return ((slots - g) % slots + aligned * (slots // 2)) % slots


def greet(slots, chips, edges):
    g, a, q, core = positions()
    barrier = pltpu.get_barrier_semaphore()
    peers = [((g + d) % slots, a) for d in range(1, slots)]
    peers += [(g, 2 * q + 1 - core)]
    peers += [(g, 2 * ((q + m) % chips) + core) for m in range(1, chips)]
    if edges:
        across = edge_partner(g, slots)
        peers += [
            (across, 2 * ((q + m) % chips) + (core + c) % 2)
            for c in range(2) for m in range(chips) if c or m
        ]
    for space, avg in peers:
        pl.semaphore_signal(
            barrier, inc=1, device_id={"space": space, "avg": avg}, device_id_type=MESH
        )
    pl.semaphore_wait(barrier, len(peers))


def sending(slots):
    return sorted(range(1, slots), key=lambda d: (-min(d, slots - d), d))


def remote(src, dst, send, recv, space, avg):
    return pltpu.make_async_remote_copy(
        src_ref=src, dst_ref=dst, send_sem=send, recv_sem=recv,
        device_id={"space": space, "avg": avg}, device_id_type=MESH,
    )


DIMS_NT = (((1,), (1,)), ((), ()))


def step_kernel(
    dims, state, into_rows, back_rows, info, ky, own_kx, phase, blocks, steps, fines, packed_hbm, result,
    moved, top, gx, eg, rows_c, rows_s, half, arr, arr_t, grid, products, packed, ct, st, sine, cosine,
    end_sine, end_cosine, fh, ret, lhs, stage, rsin, acc, xs, rx, fin, own, other, edge,
    ex_s, ex_r, eg_s, eg_r, x_s, x_r, c_s, c_r, a_s, a_r, l_s,
    b_s, b_r, m_s, d_s, d_r, y_s, y_r, gv_s, gv_r, le_s, le_r, bring_s,
):
    slots, chips, chunks, hb, width, block = dims
    length, reach = slots * block, block // 2
    g, a, q, core = positions()
    low, high = g < slots // 2, g >= slots // 2
    partner = 2 * q + 1 - core
    across = edge_partner(g, slots)
    side = g // (slots // 2)
    bring = pltpu.make_async_copy(packed_hbm, packed, bring_s)

    for f in range(3):
        for i in range(2):
            plane = state[f, i].astype(jnp.bfloat16)
            top[f, i] = plane[:EDGE]
            picked = jnp.dot(into_rows[side], plane, preferred_element_type=jnp.float32)
            picked = picked.astype(jnp.bfloat16)
            for s in range(2):
                for t in range(chunks):
                    spot = s * reach + t * hb
                    moved[s, t, f, i] = picked[spot : spot + hb]
    greet(slots, chips, True)

    def build_factors(unused):
        for t in range(chunks):
            for s in range(2):
                def one(j, carry, t=t, s=s):
                    span = pl.ds(pl.multiple_of(j * 256, 256), 256)
                    factors = wave_factors(column(info, t, s), ky[:, span], phase[...])
                    sine[t, s, :, span], cosine[t, s, :, span] = factors
                    return carry
                lax.fori_loop(0, length // 256, one, 0)

    def own_factors():
        end_sine[...], end_cosine[...] = wave_factors(own_kx[...], ky[:, :width], time_step)

    def build_tables():
        for c in range(2):
            for m in range(chips):
                owner = 2 * ((q + m) % chips) + (core + c) % 2
                first = (blocks[0, pl.ds(owner, 1), :], blocks[1, pl.ds(owner, 1), :])

                def one(h, carry, j=c * chips + m, first=first):
                    begin = turned(first, (steps[0, pl.ds(h, 1), :], steps[1, pl.ds(h, 1), :]))
                    cos_rows, sin_rows = turned(begin, (fines[0], fines[1]))
                    at = pl.ds(pl.multiple_of(j * width + h * FINE, FINE), FINE)
                    ct[at, :] = cos_rows.astype(jnp.bfloat16)
                    st[at, :] = sin_rows.astype(jnp.bfloat16)
                    return carry
                lax.fori_loop(0, width // FINE, one, 0)

    exchange = [
        remote(moved.at[1, t], gx.at[t, 1, 0, 0], ex_s.at[t], ex_r.at[t], slots - 1 - g, a)
        for t in range(chunks)
    ]
    edges = [
        remote(top, eg.at[c, m], eg_s.at[c, m], eg_r.at[c, m],
               across, 2 * ((q + chips - m) % chips) + (core + c) % 2)
        for c in range(2) for m in range(chips)
    ]

    def mine(t, s):
        return gx.at[t, 1, 0, 0] if s else moved.at[0, t]

    def over_chips(t, s, m):
        return remote(mine(t, s), gx.at[t, s, 0, m], x_s.at[t, s, m], x_r.at[t, s, m],
                      g, 2 * ((q + chips - m) % chips) + core)

    def over_cores(t, s, m):
        source = gx.at[t, s, 0, m] if m else mine(t, s)
        return remote(source, gx.at[t, s, 1, m], c_s.at[t, s, m], c_r.at[t, s, m], g, partner)

    def to_grid(t, d):
        to = (g + d) % slots
        return remote(half.at[t, to], arr.at[t, g], a_s.at[t, d], a_r.at[t, d], to, a)

    exchange[0].start()

    @pl.when(high)
    def _():
        for copy in edges:
            copy.start()
        eg[...] = jnp.zeros_like(eg)

    for t in range(1, chunks):
        exchange[t].start()
    for t in range(chunks):
        for m in range(1, chips):
            over_chips(t, 0, m).start()
        over_cores(t, 0, 0).start()
    bring.start()
    build_factors(0)
    build_tables()
    for t in range(chunks):
        for m in range(1, chips):
            over_chips(t, 0, m).wait_recv()
            over_cores(t, 0, m).start()
    def spread(t):
        exchange[t].wait_recv()
        for m in range(1, chips):
            over_chips(t, 1, m).start()
        over_cores(t, 1, 0).start()

    spread(0)
    for t in range(chunks):
        for m in range(1, chips):
            over_chips(t, 1, m).wait_recv()
            over_cores(t, 1, m).start()
        if t + 1 < chunks:
            spread(t + 1)
        if t == 0:
            @pl.when(low)
            def _():
                for copy in edges:
                    copy.wait_recv()
        for s in range(2):
            for m in range(chips):
                over_cores(t, s, m).wait_recv()
        own_pair = column(info, t, 2) > 0.5
        sign = column(info, t, 3)
        for j in range(2 * chips):
            c, m = divmod(j, chips)
            span = slice(j * width, (j + 1) * width)
            turned_rows = []
            for s in range(2):
                source = moved.at[0, t] if s + j == 0 else gx.at[t, s, c, m]
                fields = [[source[f, i].astype(jnp.float32) for i in range(2)] for f in range(3)]
                if s == 1 and t == 0:
                    put = column(info, t, 4)[:EDGE] > 0.5
                    for f in range(3):
                        for i in range(2):
                            top = jnp.where(put, eg[c, m, f, i].astype(jnp.float32), fields[f][i][:EDGE])
                            fields[f][i] = (
                                jnp.concatenate([top, fields[f][i][EDGE:]], axis=0) if hb > EDGE else top
                            )
                turned_rows.append(wave_exponential(
                    fields, column(info, t, s), ky[:, span], (sine[t, s, :, span], cosine[t, s, :, span])
                ))
            for f in range(3):
                (re0, im0), (re1, im1) = turned_rows[0][f], turned_rows[1][f]
                for i, value in enumerate((
                    jnp.where(own_pair, re0, re0 + re1), jnp.where(own_pair, re1, sign * (im0 - im1))
                )):
                    rows_c[(i * 3 + f) * hb : (i * 3 + f + 1) * hb, span] = value.astype(jnp.bfloat16)
                for i, value in enumerate((
                    jnp.where(own_pair, -im0, -(im0 + im1)), jnp.where(own_pair, -im1, sign * (re0 - re1))
                )):
                    rows_s[(i * 3 + f) * hb : (i * 3 + f + 1) * hb, span] = value.astype(jnp.bfloat16)
        tile = min(length, max(block, 256))
        for y in range(0, length, tile):
            value = (
                jnp.dot(rows_c[...], ct[:, y : y + tile], preferred_element_type=jnp.float32)
                + jnp.dot(rows_s[...], st[:, y : y + tile], preferred_element_type=jnp.float32)
            ).astype(jnp.bfloat16)
            for b in range(tile // block):
                for i in range(2):
                    for f in range(3):
                        half[t, y // block + b, i * hb : (i + 1) * hb, f * block : (f + 1) * block] = (
                            value[(i * 3 + f) * hb : (i * 3 + f + 1) * hb, b * block : (b + 1) * block]
                        )
        for d in sending(slots):
            to_grid(t, d).start()
        pltpu.make_async_copy(half.at[t, g], arr.at[t, g], l_s.at[t]).start()
    def to_rows(t, d):
        to = (g + d) % slots
        return remote(fh.at[t, to], ret.at[t, g], b_s.at[t, d], b_r.at[t, d], to, a)

    def sum_cores(t):
        return remote(stage.at[t, 1], rsin.at[t], d_s.at[t], d_r.at[t], g, partner)

    def sum_chips(t, m):
        return remote(xs.at[t, m], rx.at[t, m], y_s.at[t, m], y_r.at[t, m],
                      g, 2 * ((q + m) % chips) + core)

    def give(t):
        return remote(fin.at[t], other.at[t], gv_s.at[t], gv_r.at[t], slots - 1 - g, a)

    last = remote(fin.at[0, :, :, :EDGE], edge, le_s, le_r, edge_partner(g, slots), a)

    bring.wait()
    for t in range(chunks):
        for d in range(1, slots):
            to_grid(t, d).wait_recv()
        pltpu.make_async_copy(half.at[t, g], arr.at[t, g], l_s.at[t]).wait()
        together = max(1, 128 // (2 * hb))
        for p in range(0, slots, together):
            value = arr[t, p : p + together].astype(jnp.float32)
            value = value.reshape(together * 2 * hb, 3 * block)
            spot = p * 2 * hb
            arr_t[:, spot : spot + together * 2 * hb] = value.T.astype(jnp.bfloat16)
        depth = length // chunks
        for x in range(0, length, 256):
            value = jnp.dot(
                arr_t[...], packed[t * depth : (t + 1) * depth, x : x + 256],
                preferred_element_type=jnp.float32,
            )
            if t:
                value = value + grid[:, x : x + 256]
            if t < chunks - 1:
                grid[:, x : x + 256] = value
            else:
                value = value * (1.0 / length)
                east, north, height = (value[i * block : (i + 1) * block] for i in range(3))
                for k, pair in enumerate((
                    east * east, east * north, north * north, east * height, north * height
                )):
                    products[k * block : (k + 1) * block, x : x + 256] = pair.astype(jnp.bfloat16)
    for t in range(chunks):
        for k in range(0, depth, 256):
            value = lax.dot_general(
                packed[t * depth + k : t * depth + k + 256, :], products[...], DIMS_NT,
                preferred_element_type=jnp.float32,
            ).astype(jnp.bfloat16)
            for n in range(256 // (2 * hb)):
                fh[t, k // (2 * hb) + n] = value[n * 2 * hb : (n + 1) * 2 * hb]
        for d in sending(slots):
            to_rows(t, d).start()
        pltpu.make_async_copy(fh.at[t, g], ret.at[t, g], m_s.at[t]).start()
    own_factors()

    @pl.when(low)
    def _():
        edge[...] = jnp.zeros_like(edge)

    def finish(t):
        for m in range(1, chips):
            sum_chips(t, m).wait_recv()
            acc[...] += rx[t, m].astype(jnp.float32)
        fin[t] = acc[1].astype(jnp.bfloat16)
        give(t).start()
        if t == 0:
            @pl.when(low)
            def _():
                last.start()
        own[t] = acc[0].astype(jnp.bfloat16)

    for t in range(chunks):
        for d in range(1, slots):
            to_rows(t, d).wait_recv()
        pltpu.make_async_copy(fh.at[t, g], ret.at[t, g], m_s.at[t]).wait()
        for p in range(slots):
            for k in range(5):
                lhs[k * 2 * hb : (k + 1) * 2 * hb, p * block : (p + 1) * block] = (
                    ret[t, p, :, k * block : (k + 1) * block]
                )
        own_pair = column(info, t, 2) > 0.5
        sign, scale = column(info, t, 3), column(info, t, 5)
        for j in range(2 * chips):
            c, m = divmod(j, chips)
            span = slice(j * width, (j + 1) * width)
            by_c = lax.dot_general(lhs[...], ct[span, :], DIMS_NT, preferred_element_type=jnp.float32)
            by_s = lax.dot_general(lhs[...], st[span, :], DIMS_NT, preferred_element_type=jnp.float32)

            def part(values, k, i):
                return values[(2 * k + i) * hb : (2 * k + i + 1) * hb]

            for s in range(2):
                turn = scale * sign if s == 0 else -scale * sign
                real, imag = [], []
                for k in range(5):
                    rc, ic = part(by_c, k, 0), part(by_c, k, 1)
                    rs, iz = part(by_s, k, 0), part(by_s, k, 1)
                    real.append(jnp.where(own_pair, scale * (ic if s else rc), scale * rc + turn * iz))
                    imag.append(jnp.where(own_pair, -scale * (iz if s else rs), turn * ic - scale * rs))
                kx, kyj = column(info, t, s), ky[:, span]
                tendency = [
                    (kx * imag[u] + kyj * imag[v], -(kx * real[u] + kyj * real[v]))
                    for u, v in ((0, 1), (1, 2), (3, 4))
                ]
                back = wave_exponential(
                    tendency, kx, kyj, (-sine[t, s, :, span], cosine[t, s, :, span])
                )
                for f in range(3):
                    for i in range(2):
                        stage[t, c, m, s, f, i] = back[f][i].astype(jnp.bfloat16)
        sum_cores(t).start()
        if t:
            finish(t - 1)
        sum_cores(t).wait_recv()
        for m in range(1, chips):
            xs[t, m] = (
                stage[t, 0, m].astype(jnp.float32) + rsin[t, m].astype(jnp.float32)
            ).astype(jnp.bfloat16)
            sum_chips(t, m).start()
        acc[...] = stage[t, 0, 0].astype(jnp.float32) + rsin[t, 0].astype(jnp.float32)
    finish(chunks - 1)
    for t in range(chunks):
        give(t).wait_recv()

    @pl.when(high)
    def _():
        last.wait_recv()

    for t in range(chunks):
        exchange[t].wait_send()
        for s in range(2):
            for m in range(1, chips):
                over_chips(t, s, m).wait_send()
            for m in range(chips):
                over_cores(t, s, m).wait_send()
        for d in range(1, slots):
            to_grid(t, d).wait_send()

    @pl.when(high)
    def _():
        for copy in edges:
            copy.wait_send()


    for t in range(chunks):
        for d in range(1, slots):
            to_rows(t, d).wait_send()
        sum_cores(t).wait_send()
        for m in range(1, chips):
            sum_chips(t, m).wait_send()
        give(t).wait_send()

    @pl.when(low)
    def _():
        last.wait_send()


    for f in range(3):
        for i in range(2):
            rows = jnp.concatenate(
                [own[t, f, i] for t in range(chunks)] + [other[t, f, i] for t in range(chunks)]
                + [edge[f, i]], axis=0,
            )
            averaged = jnp.dot(back_rows[side], rows, preferred_element_type=jnp.float32)
            result[f, i] = state[f, i] + time_step * averaged
    fields = [[result[f, i] for i in range(2)] for f in range(3)]
    advanced = wave_exponential(fields, own_kx[...], ky[:, :width], (end_sine[...], end_cosine[...]))
    for f in range(3):
        for i in range(2):
            result[f, i] = advanced[f][i]


VMEM = pl.BlockSpec(memory_space=pltpu.VMEM)


def per_device(spectral_state, phase_index, weight_count):
    slots, owners = lax.axis_size("space"), lax.axis_size("avg")
    block, width = spectral_state.shape[2:]
    length, half = block * slots, block // 2
    chips = owners // 2
    chunks = max(1, half // CHUNK_ROWS)
    hb = half // chunks
    dims = (slots, chips, chunks, hb, width, block)
    g, a = lax.axis_index("space"), lax.axis_index("avg")
    q, core = a // 2, a % 2
    low = g < slots // 2
    phase = phase_index[0].astype(jnp.float32) * phase_step
    weight = weight_count[0].astype(jnp.float32) / (weight_scale * owners)

    m, c = jnp.arange(chips, dtype=jnp.int32), jnp.arange(2, dtype=jnp.int32)[:, None]
    order = (2 * ((q + m) % chips) + (core + c) % 2).reshape(-1)
    columns = (order[:, None] * width + jnp.arange(width, dtype=jnp.int32)).reshape(1, -1)
    ky = wave_of(columns, length)
    packed = jnp.asarray(packed_table(length, slots, chunks))

    base = jnp.where(low, 2 * half * g, 2 * half * (slots - 1 - g) + half)
    direct = base + jnp.arange(half, dtype=jnp.int32)
    mirror = jnp.where(direct == 0, length // 2, length - direct)
    first = wave_of(jnp.where(low, direct, mirror), length)
    second = wave_of(jnp.where(low, mirror, direct), length)
    ones = jnp.ones((half,), jnp.float32)
    start = (jnp.arange(half) == 0) & low
    info = jnp.stack([
        first, second, (direct == 0).astype(jnp.float32), jnp.where(low, ones, -ones),
        start.astype(jnp.float32), ones * (weight / length), ones, ones,
    ], axis=1).reshape(chunks, hb, 8)
    own_kx = wave_of(g * block + jnp.arange(block, dtype=jnp.int32)[:, None], length)

    r = np.arange(half)
    into = np.zeros((2, 2, half, block), np.float32)
    into[0, 0, r, r] = 1
    into[0, 1, r, half + r] = 1
    into[1, 0, r, half - r] = 1
    into[1, 1, r[1:], block - r[1:]] = 1
    into = jnp.asarray(into.reshape(2, block, block).astype(ml_dtypes.bfloat16))
    back = np.zeros((2, block, 2 * half + EDGE), np.float32)
    back[0, r, r] = 1
    back[0, half + r, half + r] = 1
    back[1, half - r, r] = 1
    back[1, block - r[1:], half + r[1:]] = 1
    back[1, 0, 2 * half] = 1
    back = jnp.asarray(back.astype(ml_dtypes.bfloat16))

    piece = (3, 2, hb, width)
    dma = pltpu.SemaphoreType.DMA
    vmem = lambda *shape: pltpu.VMEM(shape, jnp.bfloat16)
    wide = lambda *shape: pltpu.VMEM(shape, jnp.float32)
    return pl.pallas_call(
        functools.partial(step_kernel, dims),
        out_shape=jax.ShapeDtypeStruct(spectral_state.shape, jnp.float32),
        in_specs=[VMEM] * 10 + [pl.BlockSpec(memory_space=pl.ANY)],
        out_specs=VMEM,
        scratch_shapes=[
            vmem(2, chunks, *piece), vmem(3, 2, EDGE, width),
            vmem(chunks, 2, 2, chips, *piece), vmem(2, chips, 3, 2, EDGE, width),
            vmem(6 * hb, length), vmem(6 * hb, length),
            vmem(chunks, slots, 2 * hb, 3 * block), vmem(chunks, slots, 2 * hb, 3 * block),
            vmem(3 * block, length // chunks), wide(3 * block, length), vmem(5 * block, length),
            vmem(length, length), vmem(length, length), vmem(length, length),
            wide(chunks, 2, hb, length), wide(chunks, 2, hb, length),
            wide(block, width), wide(block, width),
            vmem(chunks, slots, 2 * hb, 5 * block), vmem(chunks, slots, 2 * hb, 5 * block),
            vmem(10 * hb, length),
            vmem(chunks, 2, chips, 2, *piece), vmem(chunks, chips, 2, *piece),
            wide(2, *piece), vmem(chunks, chips, 2, *piece), vmem(chunks, chips, 2, *piece),
            vmem(chunks, *piece), vmem(chunks, *piece), vmem(chunks, *piece),
            vmem(3, 2, EDGE, width),
            dma((chunks,)), dma((chunks,)),
            dma((2, chips)), dma((2, chips)),
            dma((chunks, 2, chips)), dma((chunks, 2, chips)),
            dma((chunks, 2, chips)), dma((chunks, 2, chips)),
            dma((chunks, slots)), dma((chunks, slots)), dma((chunks,)),
            dma((chunks, slots)), dma((chunks, slots)), dma((chunks,)),
            dma((chunks,)), dma((chunks,)),
            dma((chunks, chips)), dma((chunks, chips)),
            dma((chunks,)), dma((chunks,)),
            dma(()), dma(()), dma(()),
        ],
        compiler_params=pltpu.CompilerParams(
            collective_id=0, has_side_effects=True, vmem_limit_bytes=56 * 2**20
        ),
        name="averaged_step",
    )(spectral_state, into, back, info, ky, own_kx, phase.reshape(1, 1),
      *angle_tables(length, width, owners), packed)


def signal_all(barrier, peers):
    for space, avg in peers:
        pl.semaphore_signal(
            barrier, inc=1, device_id={"space": space, "avg": avg}, device_id_type=MESH
        )


def only_row(n, value, rows):
    spot = lax.broadcasted_iota(jnp.int32, (rows, value.shape[-1]), 0)
    return jnp.where(spot == n, jnp.broadcast_to(value, (rows, value.shape[-1])), 0.0)


def cube_kernel(
    dims, phase_ref, weight_ref, state_hbm, table_hbm, result,
    state, order_rows, order_part, info, ky, own_kx, parts, ph_mine, ph_got, moved, top, gx, eg, rows_c, rows_s, half, arr, arr_t, grid, products, packed,
    ct, st, sine, cosine, end_sine, end_cosine, fh, ret, lhs, stage, rsin, xs, rb, lt, le,
    ph_s, ph_r, x_s, x_r, c_s, c_r, g_s, eg_s, eg_r, a_s, a_r, l_s,
    b_s, b_r, m_s, d_s, d_r, y_s, y_r, k_s, le_s, le_r, load_s,
):
    slots, chunks, hb, width, block = dims
    length, reach = slots * block, block // 2
    g, a, q, core = positions()
    side = g // (slots // 2)
    pair_block = g + side * (slots - 1 - 2 * g)
    me = 2 * pair_block + q
    mirror = slots - 1 - g
    partner = 2 * q + 1 - core
    low, high = side == 0, side == 1

    def place(slot):
        b = slot // 2
        return b + side * (slots - 1 - 2 * b), 2 * (slot % 2) + core

    def chip(m):
        return (q + m) % 2

    barrier = pltpu.get_barrier_semaphore()
    near = [place((me + d) % slots) for d in range(1, slots)] + [(g, partner)]
    near += [(mirror, 2 * chip(m) + core) for m in range(2)]
    across = edge_partner(g, slots)
    below = [(across, c) for c in range(2)] + [(slots - 1 - across, c) for c in range(2)]
    source = edge_partner(pair_block, slots)
    above = [(source, c) for c in range(4)]
    signal_all(barrier, near)

    @pl.when(high)
    def _():
        signal_all(barrier, below)

    @pl.when(q == 0)
    def _():
        signal_all(barrier, above)
    loads = [
        pltpu.make_async_copy(source_ref, target, load_s.at[n])
        for n, (source_ref, target) in enumerate((
            (state_hbm, state), (table_hbm, parts)
        ))
    ]
    for copy in loads:
        copy.start()

    def wave(spot):
        return jnp.where(spot >= length // 2, spot - length, spot).astype(jnp.float32) * (2.0 / length)

    lane = lax.broadcasted_iota(jnp.int32, (hb, 128), 1)
    for t in range(chunks):
        spot = lax.broadcasted_iota(jnp.int32, (hb, 128), 0) + t * hb
        direct = spot + (block * pair_block + reach * q)
        mirrored = jnp.where(direct == 0, length // 2, length - direct)
        begins = jnp.where(spot == 0, 1.0, 0.0)
        info[t] = jnp.where(lane == 0, wave(direct), jnp.where(lane == 1, wave(mirrored), jnp.where(
            lane == 2, jnp.where(direct == 0, 1.0, 0.0), jnp.where(
                lane == 3, begins * (1 - q).astype(jnp.float32), begins * side.astype(jnp.float32)
            )
        )))
    own_kx[...] = wave(lax.broadcasted_iota(jnp.int32, (block, 128), 0) + g * block)
    for j in range(4):
        c, m = divmod(j, 2)
        owner = 2 * ((q + m) % 2) + (core + c) % 2
        spot = lax.broadcasted_iota(jnp.int32, (1, width), 1) + owner * width
        ky[:, j * width : (j + 1) * width] = wave(spot)
    down = lax.broadcasted_iota(jnp.int32, (block, block), 0)
    along = lax.broadcasted_iota(jnp.int32, (block, block), 1)
    turned_down = jnp.where(down == 0, 0, block - down)
    order_rows[...] = jnp.where(
        along == down + side * (turned_down - down), 1.0, 0.0
    ).astype(jnp.bfloat16)
    down = lax.broadcasted_iota(jnp.int32, (block, 2 * hb), 0)
    along = lax.broadcasted_iota(jnp.int32, (block, 2 * hb), 1)
    moved_down = down + side * (jnp.where(down == 0, 0, block - down) - down)
    for t in range(chunks):
        spot = along + t * hb + (along // hb) * (reach - hb)
        order_part[t] = jnp.where(spot == moved_down, 1.0, 0.0).astype(jnp.bfloat16)
    lane = lax.broadcasted_iota(jnp.int32, ph_mine.shape, 1)
    ph_mine[...] = jnp.where(
        lane == 0, phase_ref[0].astype(jnp.float32) * phase_step,
        weight_ref[0].astype(jnp.float32) / (weight_scale * 4),
    )
    loads[0].wait()

    top_tile = jnp.zeros((EDGE, width), jnp.float32)
    for f in range(3):
        for i in range(2):
            plane = state[f, i].astype(jnp.bfloat16)
            top_tile = top_tile + only_row(2 * f + i, state[f, i, 0:1, :], EDGE)
            picked = jnp.dot(order_rows[...], plane, preferred_element_type=jnp.float32)
            picked = picked.astype(jnp.bfloat16)
            for h in range(2):
                for t in range(chunks):
                    spot = h * reach + t * hb
                    moved[h, t, f, i] = picked[spot : spot + hb]
    top[...] = top_tile.astype(jnp.bfloat16)
    pl.semaphore_wait(barrier, len(near) + len(below) * side + len(above) * (1 - q))

    def build_factors(t):
        turn = chosen_phase()[:, 0:1]
        if True:
            for s in range(2):
                def one(j, carry, t=t, s=s):
                    span = pl.ds(pl.multiple_of(j * 256, 256), 256)
                    factors = wave_factors(column(info, t, s), ky[:, span], turn)
                    sine[t, s, :, span], cosine[t, s, :, span] = factors
                    return carry
                lax.fori_loop(0, length // 256, one, 0)

    def chosen_phase():
        keep = 1.0 - jnp.abs(q - side).astype(jnp.float32)
        return ph_got[0:1] + keep * (ph_mine[0:1] - ph_got[0:1])

    steps, owners = width // FINE, 4

    def begin_rows(owner, h):
        return turned(
            (parts[pl.ds(2 * (FINE + steps) + owner, 1)], parts[pl.ds(2 * (FINE + steps) + owners + owner, 1)]),
            (parts[pl.ds(2 * FINE + h, 1)], parts[pl.ds(2 * FINE + steps + h, 1)]),
        )

    def fine_rows(begin):
        return turned(begin, (parts[0:FINE], parts[FINE : 2 * FINE]))

    def build_packed():
        def one(n, carry):
            begin = begin_rows(n // steps, n % steps)
            cos_rows, sin_rows = fine_rows(begin)
            slot, t = n // chunks, n % chunks
            at = pl.multiple_of((t * slots + slot) * 2 * hb, 2 * hb)
            packed[pl.ds(at, hb), :] = cos_rows.astype(jnp.bfloat16)
            packed[pl.ds(at + hb, hb), :] = (-sin_rows).astype(jnp.bfloat16)
            return carry
        lax.fori_loop(0, length // (2 * FINE), one, 0)
        down = lax.broadcasted_iota(jnp.int32, (hb, length), 0)
        along = lax.broadcasted_iota(jnp.int32, (hb, length), 1)
        rest = packed[hb : 2 * hb, :].astype(jnp.float32)
        packed[hb : 2 * hb, :] = jnp.where(
            down == 0, 1.0 - 2.0 * (along % 2).astype(jnp.float32), rest
        ).astype(jnp.bfloat16)

    def build_tables():
        for c in range(2):
            for m in range(2):
                owner = 2 * chip(m) + (core + c) % 2

                def one(h, carry, j=c * 2 + m, owner=owner):
                    cos_rows, sin_rows = fine_rows(begin_rows(owner, h))
                    at = pl.ds(pl.multiple_of(j * width + h * FINE, FINE), FINE)
                    ct[at, :] = cos_rows.astype(jnp.bfloat16)
                    st[at, :] = sin_rows.astype(jnp.bfloat16)
                    return carry
                lax.fori_loop(0, width // FINE, one, 0)

    swap_phase = remote(ph_mine, ph_got, ph_s, ph_r, g, 2 * chip(1) + core)

    def bring_own(t):
        return remote(moved.at[chip(1), t], gx.at[t, side, 0, 1], x_s.at[t, 0], x_r.at[t, 0],
                      g, 2 * chip(1) + core)

    def bring_mirror(t, m):
        return remote(moved.at[chip(m), t], gx.at[t, side, 0, m], x_s.at[t, 1 + m], x_r.at[t, 1 + m],
                      mirror, 2 * chip(m) + core)

    def keep_own(t):
        return pltpu.make_async_copy(moved.at[q, t], gx.at[t, side, 0, 0], g_s.at[t])

    def over_cores(t, kind, m):
        role = (1 - side) if kind else side
        piece = gx.at[t, role, 0, m] if kind + m else moved.at[q, t]
        return remote(piece, gx.at[t, role, 1, m], c_s.at[t, kind, m], c_r.at[t, kind, m], g, partner)

    edges = [
        remote(top, eg.at[c, q], eg_s.at[k, c], eg_r.at[c, q], space, (core + c) % 2)
        for k, space in enumerate((across, slots - 1 - across)) for c in range(2)
    ]

    def to_grid(t, d):
        to = (me + d) % slots
        space, avg = place(to)
        return remote(half.at[t, to], arr.at[t, me], a_s.at[t, d], a_r.at[t, d], space, avg)

    def to_rows(t, d):
        to = (me + d) % slots
        space, avg = place(to)
        return remote(fh.at[t, to], ret.at[t, me], b_s.at[t, d], b_r.at[t, d], space, avg)

    def sum_cores(t):
        return remote(stage.at[t, 1], rsin.at[t], d_s.at[t], d_r.at[t], g, partner)

    def give_own(t):
        return remote(xs.at[t, 1, side], rb.at[t, 0, q], y_s.at[t, 0], y_r.at[t, 0],
                      g, 2 * chip(1) + core)

    def give_mirror(t, m):
        return remote(xs.at[t, m, 1 - side], rb.at[t, 1, q], y_s.at[t, 1 + m], y_r.at[t, 1 + m],
                      mirror, 2 * chip(m) + core)

    def give_self(t):
        return pltpu.make_async_copy(xs.at[t, 0, side], rb.at[t, 0, q], k_s.at[t])

    last = [
        remote(lt.at[m], le.at[side], le_s.at[m], le_r.at[side], source, 2 * chip(m) + core)
        for m in range(2)
    ]

    swap_phase.start()

    @pl.when(high)
    def _():
        for copy in edges:
            copy.start()
    def launch(t):
        for m in range(2):
            bring_mirror(t, m).start()
        bring_own(t).start()
        over_cores(t, 0, 0).start()
        keep_own(t).start()

    launch(0)
    pass
    @pl.when(q != 0)
    def _():
        eg[...] = jnp.zeros_like(eg)

    @pl.when(low)
    def _():
        le[...] = jnp.zeros_like(le)
    swap_phase.wait_recv()
    scale = chosen_phase()[:, 1:2] * (1.0 / length)

    def meet_edges():
        @pl.when(q == 0)
        def _():
            for c in range(2):
                for m in range(2):
                    remote(top, eg.at[c, m], eg_s.at[0, c], eg_r.at[c, m], g, partner).wait_recv()

    def rotate(t):
        bring_own(t).wait_recv()
        over_cores(t, 0, 1).start()
        for m in range(2):
            bring_mirror(t, m).wait_recv()
            over_cores(t, 1, m).start()
        keep_own(t).wait()
        for kind in range(2):
            for m in range(2):
                over_cores(t, kind, m).wait_recv()
        own_pair = column(info, t, 2) > 0.5
        for j in range(4):
            c, m = divmod(j, 2)
            span = slice(j * width, (j + 1) * width)
            turned_rows = []
            for s in range(2):
                piece = gx.at[t, s, c, m]
                fields = [[piece[f, i].astype(jnp.float32) for i in range(2)] for f in range(3)]
                if s == 1 and t == 0:
                    put = column(info, t, 3) > 0.5
                    tile = eg[c, m].astype(jnp.float32)
                    for f in range(3):
                        for i in range(2):
                            n = 2 * f + i
                            row = jnp.broadcast_to(tile[n : n + 1], (hb, width))
                            fields[f][i] = jnp.where(put, row, fields[f][i])
                turned_rows.append(wave_exponential(
                    fields, column(info, t, s), ky[:, span], (sine[t, s, :, span], cosine[t, s, :, span])
                ))
            for f in range(3):
                (re0, im0), (re1, im1) = turned_rows[0][f], turned_rows[1][f]
                for i, value in enumerate((
                    jnp.where(own_pair, re0, re0 + re1), jnp.where(own_pair, re1, im0 - im1)
                )):
                    rows_c[(i * 3 + f) * hb : (i * 3 + f + 1) * hb, span] = value.astype(jnp.bfloat16)
                for i, value in enumerate((
                    jnp.where(own_pair, -im0, -(im0 + im1)), jnp.where(own_pair, -im1, re0 - re1)
                )):
                    rows_s[(i * 3 + f) * hb : (i * 3 + f + 1) * hb, span] = value.astype(jnp.bfloat16)
        tile = min(length, max(block, 256))
        for y in range(0, length, tile):
            value = (
                jnp.dot(rows_c[...], ct[:, y : y + tile], preferred_element_type=jnp.float32)
                + jnp.dot(rows_s[...], st[:, y : y + tile], preferred_element_type=jnp.float32)
            ).astype(jnp.bfloat16)
            for b in range(tile // block):
                for i in range(2):
                    for f in range(3):
                        half[t, y // block + b, i * hb : (i + 1) * hb, f * block : (f + 1) * block] = (
                            value[(i * 3 + f) * hb : (i * 3 + f + 1) * hb, b * block : (b + 1) * block]
                        )
        for d in sending(slots):
            to_grid(t, d).start()
        pltpu.make_async_copy(half.at[t, me], arr.at[t, me], l_s.at[t]).start()

    depth = length // chunks

    def send_rows(t):
        for d in sending(slots):
            to_rows(t, d).start()
        pltpu.make_async_copy(fh.at[t, me], ret.at[t, me], m_s.at[t]).start()

    def on_grid(t):
        for d in range(1, slots):
            to_grid(t, d).wait_recv()
        pltpu.make_async_copy(half.at[t, me], arr.at[t, me], l_s.at[t]).wait()
        together = max(1, 128 // (2 * hb))
        for p in range(0, slots, together):
            value = arr[t, p : p + together].astype(jnp.float32)
            value = value.reshape(together * 2 * hb, 3 * block)
            spot = p * 2 * hb
            arr_t[:, spot : spot + together * 2 * hb] = value.T.astype(jnp.bfloat16)
        for x in range(0, length, 256):
            value = jnp.dot(
                arr_t[...], packed[t * depth : (t + 1) * depth, x : x + 256],
                preferred_element_type=jnp.float32,
            )
            if t:
                value = value + grid[:, x : x + 256]
            if t < chunks - 1:
                grid[:, x : x + 256] = value
            else:
                value = value * (1.0 / length)
                east, north, height = (value[i * block : (i + 1) * block] for i in range(3))
                for k, pair in enumerate((
                    east * east, east * north, north * north, east * height, north * height
                )):
                    products[k * block : (k + 1) * block, x : x + 256] = pair.astype(jnp.bfloat16)

    loads[1].wait()
    build_tables()
    build_factors(0)
    launch(1)
    build_factors(1)
    meet_edges()
    rotate(0)
    launch(2)
    build_packed()
    build_factors(2)
    rotate(1)
    launch(3)
    on_grid(0)
    build_factors(3)
    rotate(2)
    on_grid(1)
    rotate(3)
    on_grid(2)
    end_sine[...], end_cosine[...] = wave_factors(own_kx[:, 0:1], ky[:, :width], time_step)
    on_grid(chunks - 1)

    for t in range(chunks):
        for k in range(0, depth, 256):
            value = lax.dot_general(
                packed[t * depth + k : t * depth + k + 256, :], products[...], DIMS_NT,
                preferred_element_type=jnp.float32,
            ).astype(jnp.bfloat16)
            for n in range(256 // (2 * hb)):
                fh[t, k // (2 * hb) + n] = value[n * 2 * hb : (n + 1) * 2 * hb]
        if t == 0:
            send_rows(0)
        if t == min(2, chunks - 1) and chunks > 1:
            send_rows(1)

    def pass_on(t):
        sum_cores(t).wait_recv()
        for m in range(2):
            for s in range(2):
                value = stage[t, 0, m, s].astype(jnp.float32) + rsin[t, m, s].astype(jnp.float32)
                xs[t, m, s] = value.astype(jnp.bfloat16)
                if t == 0 and s == 1:
                    tile = jnp.zeros((EDGE, width), jnp.float32)
                    for f in range(3):
                        for i in range(2):
                            tile = tile + only_row(2 * f + i, value[f, i, 0:1], EDGE)
                    lt[m] = tile.astype(jnp.bfloat16)
            give_mirror(t, m).start()
        give_own(t).start()
        give_self(t).start()
        if t == 0:
            @pl.when(q == 0)
            def _():
                for copy in last:
                    copy.start()

    for t in range(chunks):
        for d in range(1, slots):
            to_rows(t, d).wait_recv()
        pltpu.make_async_copy(fh.at[t, me], ret.at[t, me], m_s.at[t]).wait()
        if t + 2 < chunks:
            send_rows(t + 2)
        for p in range(slots):
            for k in range(5):
                lhs[k * 2 * hb : (k + 1) * 2 * hb, p * block : (p + 1) * block] = (
                    ret[t, p, :, k * block : (k + 1) * block]
                )
        own_pair = column(info, t, 2) > 0.5
        for j in (2, 3, 0, 1):
            c, m = divmod(j, 2)
            if j == 0:
                sum_cores(t).start()
            span = slice(j * width, (j + 1) * width)
            by_c = lax.dot_general(lhs[...], ct[span, :], DIMS_NT, preferred_element_type=jnp.float32)
            by_s = lax.dot_general(lhs[...], st[span, :], DIMS_NT, preferred_element_type=jnp.float32)

            def part(values, k, i):
                return values[(2 * k + i) * hb : (2 * k + i + 1) * hb] * scale

            for s in range(2):
                real, imag = [], []
                for k in range(5):
                    rc, ic = part(by_c, k, 0), part(by_c, k, 1)
                    rs, iz = part(by_s, k, 0), part(by_s, k, 1)
                    real.append(jnp.where(own_pair, (ic if s else rc), (rc - iz if s else rc + iz)))
                    imag.append(jnp.where(own_pair, -(iz if s else rs), (-ic if s else ic) - rs))
                kx, kyj = column(info, t, s), ky[:, span]
                tendency = [
                    (kx * imag[u] + kyj * imag[v], -(kx * real[u] + kyj * real[v]))
                    for u, v in ((0, 1), (1, 2), (3, 4))
                ]
                back = wave_exponential(
                    tendency, kx, kyj, (-sine[t, s, :, span], cosine[t, s, :, span])
                )
                for f in range(3):
                    for i in range(2):
                        stage[t, c, m, s, f, i] = back[f][i].astype(jnp.bfloat16)
        pass_on(t)

    for t in range(chunks):
        bring_own(t).wait_send()
        for m in range(2):
            bring_mirror(t, m).wait_send()
        for kind in range(2):
            for m in range(2):
                over_cores(t, kind, m).wait_send()
        for d in range(1, slots):
            to_grid(t, d).wait_send()
            to_rows(t, d).wait_send()
        sum_cores(t).wait_send()
    swap_phase.wait_send()

    @pl.when(high)
    def _():
        for copy in edges:
            copy.wait_send()
        for k in range(2):
            remote(lt.at[0], le.at[k], le_s.at[0], le_r.at[k], g, partner).wait_recv()

    edge = le[0].astype(jnp.float32) + le[1].astype(jnp.float32)
    for f in range(3):
        for i in range(2):
            result[f, i] = state[f, i] * (1.0 / time_step)
    for t in range(chunks):
        give_own(t).wait_recv()
        for m in range(2):
            give_mirror(t, m).wait_recv()
        give_self(t).wait()
        for f in range(3):
            for i in range(2):
                pieces = [
                    rb[t, 0, h, f, i].astype(jnp.float32) + rb[t, 1, h, f, i].astype(jnp.float32)
                    for h in range(2)
                ]
                n = 2 * f + i
                if t == 0:
                    pieces[0] = jnp.where(
                        column(info, 0, 4) > 0.5, jnp.broadcast_to(edge[n : n + 1], (hb, width)), pieces[0]
                    )
                rows = jnp.concatenate(pieces, axis=0).astype(jnp.bfloat16)
                averaged = jnp.dot(
                    order_part[t], rows, preferred_element_type=jnp.float32
                )
                result[f, i] = result[f, i] + averaged
    fields = [[result[f, i] for i in range(2)] for f in range(3)]
    advanced = wave_exponential(fields, own_kx[:, 0:1], ky[:, :width], (end_sine[...], end_cosine[...]))
    for f in range(3):
        for i in range(2):
            result[f, i] = advanced[f][i]

    for t in range(chunks):
        give_own(t).wait_send()
        for m in range(2):
            give_mirror(t, m).wait_send()

    @pl.when(q == 0)
    def _():
        for copy in last:
            copy.wait_send()


def cube_step(spectral_state, phase_index, weight_count):
    slots, owners = lax.axis_size("space"), lax.axis_size("avg")
    block, width = spectral_state.shape[2:]
    length, half = block * slots, block // 2
    chunks = max(1, half // CHUNK_ROWS)
    hb = half // chunks
    dims = (slots, chunks, hb, width, block)
    spans = ((1, FINE), (FINE, width // FINE), (width, owners))
    table = np.concatenate([
        part for step, count in spans
        for part in circle(step * np.arange(count)[:, None] * np.arange(length), length)
    ])
    table = jnp.asarray(table)
    piece = (3, 2, hb, width)
    dma = pltpu.SemaphoreType.DMA
    vmem = lambda *shape: pltpu.VMEM(shape, jnp.bfloat16)
    wide = lambda *shape: pltpu.VMEM(shape, jnp.float32)
    return time_step * pl.pallas_call(
        functools.partial(cube_kernel, dims),
        out_shape=jax.ShapeDtypeStruct(spectral_state.shape, jnp.float32),
        in_specs=[pl.BlockSpec(memory_space=pltpu.SMEM)] * 2 + [pl.BlockSpec(memory_space=pltpu.HBM)] * 2,
        out_specs=VMEM,
        scratch_shapes=[
            wide(3, 2, block, width), vmem(block, block), vmem(chunks, block, 2 * hb), wide(chunks, hb, 128), wide(1, length),
            wide(block, 128), wide(*table.shape),
            wide(8, 128), wide(8, 128),
            vmem(2, chunks, *piece), vmem(EDGE, width),
            vmem(chunks, 2, 2, 2, *piece), vmem(2, 2, EDGE, width),
            vmem(6 * hb, length), vmem(6 * hb, length),
            vmem(chunks, slots, 2 * hb, 3 * block), vmem(chunks, slots, 2 * hb, 3 * block),
            vmem(3 * block, length // chunks), wide(3 * block, length), vmem(5 * block, length),
            vmem(length, length), vmem(length, length), vmem(length, length),
            wide(chunks, 2, hb, length), wide(chunks, 2, hb, length),
            wide(block, width), wide(block, width),
            vmem(chunks, slots, 2 * hb, 5 * block), vmem(chunks, slots, 2 * hb, 5 * block),
            vmem(10 * hb, length),
            vmem(chunks, 2, 2, 2, *piece), vmem(chunks, 2, 2, *piece),
            vmem(chunks, 2, 2, *piece), vmem(chunks, 2, 2, *piece),
            vmem(2, EDGE, width), vmem(2, EDGE, width),
            dma(()), dma(()),
            dma((chunks, 3)), dma((chunks, 3)),
            dma((chunks, 2, 2)), dma((chunks, 2, 2)), dma((chunks,)),
            dma((2, 2)), dma((2, 2)),
            dma((chunks, slots)), dma((chunks, slots)), dma((chunks,)),
            dma((chunks, slots)), dma((chunks, slots)), dma((chunks,)),
            dma((chunks,)), dma((chunks,)),
            dma((chunks, 3)), dma((chunks, 3)), dma((chunks,)),
            dma((2,)), dma((2,)), dma((2,)),
        ],
        compiler_params=pltpu.CompilerParams(
            collective_id=0, has_side_effects=True, vmem_limit_bytes=105 * 2**19
        ),
        name="averaged_step",
    )(phase_index, weight_count, spectral_state, table)


CHUNK_ROWS = 16


def solution(mesh):
    in_specs = (P(None, None, "space", "avg"), P("avg"), P("avg"))
    out_specs = P(None, None, "space", "avg")
    body = cube_step if mesh.shape["avg"] == 4 else per_device
    return jax.shard_map(
        body, mesh=mesh, in_specs=in_specs, out_specs=out_specs, check_vma=False
    )
```
